512 devices in a mesh: col: 64 (over x, z), tm: 8 (over y, core).
Axes of the slice: x: 4, y: 4, z: 16, core: 2. Of those that a mesh axis runs over, the one named last changes fastest.
Arguments:
- series: bfloat16 [1200, 98304], P(None, 'col'), may hold values from -700 to 700
- slab_series: float32 [1200, 2048], P('tm', 'col'), may hold values from -700 to 700
- phase_index: int32 [4, 600], P(None, 'tm'), may hold values from 0 to 1199
Outputs:
- tile_peak: float32 [4, 2048, 64], P(None, None, 'col')
- peak_all: float32 [4], replicated
The draws below stay inside these ranges and needn't reach their ends.
All inputs are finite; a program needn't handle non-finite values.
Results may differ from the reference program's by a relative error of at most 0.0013.
Values may be sent and summed in bfloat16 or wider, within the bound.
A program may use at most 64 MiB of HBM per device.

```python
import math
import jax
import jax.numpy as jnp
from jax import lax

FRAMES = 1200
FREQS = 600
SURR = 4
COLS_DEV = 1536
VERTS = 98304
SLAB = 2048
N_COL = 64


def rough_field(key, row_total, col_total):
    key_col, key_row, key_shift, key_noise = jax.random.split(key, 4)
    col_scale = jnp.exp(jax.random.uniform(key_col, (col_total,), jnp.float32, 0.0, math.log(10.0)))
    row_scale = jnp.exp(jax.random.uniform(key_row, (row_total,), jnp.float32, 0.0, math.log(10.0)))
    shift = jax.random.uniform(key_shift, (col_total,), jnp.float32, -2.0, 2.0)
    noise_field = jnp.clip(jax.random.normal(key_noise, (row_total, col_total), jnp.float32), -6.0, 6.0)
    return (noise_field * row_scale[:, None] + shift[None, :]) * col_scale[None, :]


def draw_series(key, part):
    return rough_field(jax.random.fold_in(key, 11), FRAMES, VERTS).astype(jnp.bfloat16)


def draw_slab_series(key, part):
    return rough_field(jax.random.fold_in(key, 23), FRAMES, SLAB).astype(jnp.float32)


def with_ends(result, key, least, top_value):
    longest = result.shape.index(max(result.shape))
    spots = []
    for shift in (0, 1):
        where = [jax.random.randint(jax.random.fold_in(key, axis), (), 0, length) for axis, length in enumerate(result.shape)]
        where[longest] = (where[longest] + shift) % result.shape[longest]
        spots.append(tuple(where))
    return result.at[spots[0]].set(least).at[spots[1]].set(top_value)


def setup_inputs(seed: int = 0) -> dict:
    key_of = jax.random.split(jax.random.key(seed), 4)
    return {
        "series": draw_series(jax.random.fold_in(key_of[3], 71), 0),
        "slab_series": draw_slab_series(jax.random.fold_in(key_of[3], 71), 0),
        "phase_index": with_ends(jax.random.randint(key_of[2], (SURR, FREQS), 0, FRAMES), jax.random.fold_in(key_of[2], 1), 0, FRAMES - 1).astype(jnp.int32),
    }


EPSILON = 1e-06
HIGHEST = lax.Precision.HIGHEST

def twiddle(frame_ids, freq_ids):
    turn_count = frame_ids[:, None] * freq_ids[None, :] % FRAMES
    angles = turn_count.astype(jnp.float32) * (2.0 * math.pi / FRAMES)
    return (jnp.cos(angles), jnp.sin(angles))

def rotate_back(spec_cos, spec_sin, phase_ids, freq_ids, cos_back, sin_back):
    phase_angle = phase_ids.astype(jnp.float32) * (2.0 * math.pi / FRAMES)
    phase_cos = jnp.cos(phase_angle)[:, :, None]
    phase_sin = jnp.sin(phase_angle)[:, :, None]
    weights = (jnp.where(freq_ids < FREQS, 2.0, 1.0) / FRAMES).astype(jnp.float32)[None, :, None]
    rot_real = (spec_cos[None] * phase_cos + spec_sin[None] * phase_sin) * weights
    rot_imag = (spec_cos[None] * phase_sin - spec_sin[None] * phase_cos) * weights
    return jnp.einsum('sfv,tf->svt', rot_real, cos_back, precision=HIGHEST) - jnp.einsum('sfv,tf->svt', rot_imag, sin_back, precision=HIGHEST)

def normalize_rows(surrogate):
    return (surrogate * lax.rsqrt(lax.optimization_barrier(jnp.sum(surrogate * surrogate, axis=2, keepdims=True)) + EPSILON)).astype(jnp.bfloat16)

def reference(series, slab_series, phase_index):
    frame_ids = jnp.arange(FRAMES, dtype=jnp.int32)
    freq_ids = jnp.arange(1, FREQS + 1, dtype=jnp.int32)
    cos_tab, sin_tab = twiddle(frame_ids, freq_ids)
    spec_cos = jnp.dot(cos_tab.T, slab_series, precision=HIGHEST)
    spec_sin = jnp.dot(sin_tab.T, slab_series, precision=HIGHEST)
    normed = normalize_rows(rotate_back(spec_cos, spec_sin, phase_index, freq_ids, cos_tab, sin_tab))
    normed_wide = normed.astype(jnp.float32)
    values = series.astype(jnp.float32)
    centered = values - lax.optimization_barrier(jnp.mean(values, axis=0, keepdims=True))
    normed_cols = (centered * lax.rsqrt(lax.optimization_barrier(jnp.sum(centered * centered, axis=0, keepdims=True)) + EPSILON)).astype(jnp.bfloat16)

    def block_peak(block_id):
        block_cols = lax.dynamic_slice_in_dim(normed_cols, block_id * COLS_DEV, COLS_DEV, 1).astype(jnp.float32)
        scores = jnp.einsum('srt,tc->src', normed_wide, block_cols)
        return lax.optimization_barrier(jnp.max(jnp.abs(scores), axis=2))
    blocks = lax.map(block_peak, jnp.arange(N_COL, dtype=jnp.int32))
    tile_peak = jnp.transpose(blocks, (1, 2, 0)) * math.sqrt(FRAMES)
    peak_all = lax.optimization_barrier(jnp.max(tile_peak, axis=(1, 2)))
    return (tile_peak, peak_all)
```

```python
import functools
import math

import jax
import jax.numpy as jnp
import numpy as np
from jax import lax
from jax.experimental import pallas as pl
from jax.experimental.pallas import tpu as pltpu
from jax.sharding import PartitionSpec as P

FRAMES = 1200
FREQS = 600
FP = 640
TP = 1280
SURR = 4
COLS = 1536
EPS = 1e-6
F32 = jnp.float32
BF16 = jnp.bfloat16
MESH = pl.DeviceIdType.MESH
NEAR = (4, -4, 3, -3, 2, -2, 1, -1)


def basis_tables():
    freq = np.arange(1, FP + 1)[:, None]
    lane = np.arange(128)[None, :]
    fine = 2.0 * np.pi * ((freq * lane) % FRAMES) / FRAMES
    step = np.broadcast_to(2.0 * np.pi * ((freq * 128) % FRAMES) / FRAMES, fine.shape)
    return np.stack([np.cos(fine), np.sin(fine), np.cos(step), np.sin(step)]).astype(np.float32)


def dot(a, b):
    return lax.dot_general(a, b, (((1,), (0,)), ((), ())), preferred_element_type=F32)


def dot_t(a, b):
    return lax.dot_general(a, b, (((1,), (1,)), ((), ())), preferred_element_type=F32)


def kernel(
    series, slab, phase, basis, out_tile, out_peak,
    cols, bas, thi, tlo, kc, held, chunks, angles, spec, rot, best, mine, parts, own_top, top1, wide_top, top2, line_top, top3,
    col_sem, bas_sem, chunk_send, chunk_recv, ang_send, ang_recv, near_send, relay_send, x_send, unit_recv,
    part_send, part_recv, t1_send, t1_recv, t2_send, t2_recv, t3_send, t3_recv,
):
    col = lax.axis_index("col")
    k = lax.axis_index("tm")
    xx = lax.div(col, 16)
    z = lax.rem(col, 16)
    residue = lax.rem(k, 4)
    half = lax.div(k, 4)
    z_low = lax.rem(z, 4)
    hub = z_low == residue

    def at_z(d):
        return (xx * 16 + lax.rem(z + d + 16, 16), k)

    def at_x(d):
        return (lax.rem(xx + d, 4) * 16 + z, k)

    def at_k(d):
        return (col, lax.rem(k + d, 8))

    def remote(src, dst, send, recv, dev):
        return pltpu.make_async_remote_copy(
            src_ref=src, dst_ref=dst, send_sem=send, recv_sem=recv, device_id=dev, device_id_type=MESH
        )

    series_copy = pltpu.make_async_copy(series, cols.at[pl.ds(0, FRAMES)], col_sem)
    basis_copy = pltpu.make_async_copy(basis, bas, bas_sem)
    basis_copy.start()
    series_copy.start()

    barrier = pltpu.get_barrier_semaphore()
    peers = [at_k(d) for d in range(1, 8)] + [at_x(d) for d in range(1, 4)] + [at_z(d) for d in NEAR]
    for dev in peers:
        pl.semaphore_signal(barrier, inc=1, device_id=dev, device_id_type=MESH)

    cols[pl.ds(FRAMES, TP - FRAMES), :] = jnp.zeros((TP - FRAMES, COLS), BF16)
    basis_copy.wait()

    def make_rows(i, _):
        at = pl.multiple_of(i * 64, 64)
        c = bas[0, pl.ds(at, 64), :]
        s = bas[1, pl.ds(at, 64), :]
        sc = bas[2, pl.ds(at, 64), :]
        ss = bas[3, pl.ds(at, 64), :]
        for a in range(10):
            lanes = pl.ds(a * 128, 128)
            for base, val in ((0, c), (FP, s)):
                hi = val.astype(BF16)
                thi[pl.ds(base + at, 64), lanes] = hi
                tlo[pl.ds(base + at, 64), lanes] = (val - hi.astype(F32)).astype(BF16)
            c, s = c * sc - s * ss, s * sc + c * ss
        return 0

    lax.fori_loop(0, 10, make_rows, 0)

    pl.semaphore_wait(barrier, 18)

    for h in range(2):
        target = h * 4 + z_low

        @pl.when(target != k)
        def _():
            remote(slab.at[pl.ds(h * 16, 16)], chunks.at[k], chunk_send.at[h], chunk_recv.at[k], (col, target)).start()

    for d in range(1, 8):
        remote(phase, angles.at[k], ang_send.at[d], ang_recv.at[k], at_k(d)).start()
    angles[k] = phase[...]

    def norm_cols(j):
        lanes = pl.ds(j * 512, 512)

        def total(i, acc):
            x = cols[pl.ds(pl.multiple_of(i * 80, 16), 80), lanes].astype(F32)
            return acc + jnp.sum(x.reshape(10, 8, 512), axis=0)

        mean = jnp.sum(lax.fori_loop(0, 15, total, jnp.zeros((8, 512), F32)), axis=0, keepdims=True) * (1.0 / FRAMES)

        def squares(i, acc):
            x = cols[pl.ds(pl.multiple_of(i * 80, 16), 80), lanes].astype(F32) - mean
            return acc + jnp.sum((x * x).reshape(10, 8, 512), axis=0)

        scale = lax.rsqrt(jnp.sum(lax.fori_loop(0, 15, squares, jnp.zeros((8, 512), F32)), axis=0, keepdims=True) + EPS)

        def write(i, _):
            rows = pl.ds(pl.multiple_of(i * 80, 16), 80)
            cols[rows, lanes] = ((cols[rows, lanes].astype(F32) - mean) * scale).astype(BF16)
            return 0

        lax.fori_loop(0, 15, write, 0)

    def transform_cols(j):
        lanes = pl.ds(j * 256, 256)

        def block(i, _):
            rows = pl.ds(pl.multiple_of(i * 256, 256), 256)
            c = cols[:, lanes]
            kc[rows, lanes] = (dot(thi[rows, :], c) + dot(tlo[rows, :], c)).astype(BF16)
            return 0

        lax.fori_loop(0, 5, block, 0)

    series_copy.wait()
    norm_cols(0)

    a_me = lax.div(z + 16 - residue, 4)
    a_me = lax.rem(a_me, 4)

    def unit(da):
        return xx * 4 + lax.rem(a_me + da + 4, 4)

    @pl.when(hub)
    def _():
        chunks[k] = slab[pl.ds(pl.multiple_of(half * 16, 16), 16), :]
        for d in range(1, 8):
            src = lax.rem(k + d, 8)
            remote(chunks.at[src], chunks.at[src], chunk_send.at[0], chunk_recv.at[src], at_k(1)).wait_recv()
        x = jnp.concatenate([chunks[i] for i in range(8)], axis=1)
        x = x - jnp.sum(x, axis=1, keepdims=True) * (1.0 / FRAMES)
        u = unit(0)
        held[u] = jnp.concatenate([x, jnp.zeros((16, TP - FRAMES), F32)], axis=1).astype(BF16)
        for n, d in enumerate(NEAR):
            remote(held.at[u], held.at[u], near_send.at[n], unit_recv.at[u], at_z(d)).start()

    for order, da in enumerate((0, 1, -1, 2)):
        u = unit(da)
        got = remote(held.at[u], held.at[u], near_send.at[0], unit_recv.at[u], at_z(1))
        if da == 0:

            @pl.when(jnp.logical_not(hub))
            def _():
                got.wait_recv()

        else:
            got.wait_recv()
        if da == 1:

            @pl.when(hub)
            def _():
                for n, d in enumerate((-3, -2, -1)):
                    remote(held.at[u], held.at[u], relay_send.at[n], unit_recv.at[u], at_z(d)).start()

        if da == -1:

            @pl.when(hub)
            def _():
                for n, d in enumerate((4, 3, 2, 1)):
                    remote(held.at[u], held.at[u], relay_send.at[3 + n], unit_recv.at[u], at_z(d)).start()

        for n, d in enumerate((2, 1, 3)):
            remote(held.at[u], held.at[u], x_send.at[order * 3 + n], unit_recv.at[u], at_x(d)).start()
        if order == 0:
            norm_cols(1)
        elif order == 1:
            norm_cols(2)
            transform_cols(0)
        elif order == 2:
            transform_cols(1)
    for j in range(2, 6):
        transform_cols(j)

    for d in range(1, 8):
        src = lax.rem(k + d, 8)
        remote(angles.at[src], angles.at[src], ang_send.at[0], ang_recv.at[src], at_k(1)).wait_recv()
    turn = jnp.concatenate([angles[i] for i in range(8)] + [jnp.zeros((SURR, FP - FREQS), jnp.int32)], axis=1)
    angle = turn.astype(F32) * (2.0 * math.pi / FRAMES)
    lane = lax.broadcasted_iota(jnp.int32, (SURR, FP), 1)
    weight = jnp.where(lane < FREQS - 1, 1.0, jnp.where(lane == FREQS - 1, 0.5, 0.0)).astype(F32)
    cos_phase = jnp.cos(angle) * weight
    sin_phase = jnp.sin(angle) * weight

    for dx in range(1, 4):
        for a in range(4):
            u = lax.rem(xx + dx, 4) * 4 + a
            remote(held.at[u], held.at[u], near_send.at[0], unit_recv.at[u], at_x(dx)).wait_recv()

    xs = held[...].reshape(256, TP)
    for j in range(5):
        rows = pl.ds(j * 256, 256)
        spec[:, rows] = dot_t(xs, thi[rows, :]) + dot_t(xs, tlo[rows, :])
    lane1 = lax.broadcasted_iota(jnp.int32, (1, FP), 1)
    inner = (lane1 < FREQS - 1).astype(F32)
    sc = spec[:, 0:FP]
    ss = spec[:, FP:TP]
    power = jnp.sum((sc * sc + ss * ss) * inner, axis=1, keepdims=True)
    last = jnp.sum(jnp.where(lane1 == FREQS - 1, sc, 0.0), axis=1, keepdims=True)
    for s in range(SURR):
        cp = cos_phase[s : s + 1, :]
        sp = sin_phase[s : s + 1, :]
        rot[pl.ds(s * 256, 256), 0:FP] = (sc * cp + ss * sp).astype(BF16)
        rot[pl.ds(s * 256, 256), FP:TP] = (ss * cp - sc * sp).astype(BF16)

    best[...] = jnp.zeros_like(best)

    def correlate(j, _):
        lanes = pl.ds(pl.multiple_of(j * 256, 256), 256)
        right = kc[:, lanes]
        for s in range(SURR):
            rows = pl.ds(s * 256, 256)
            score = jnp.abs(dot(rot[rows, :], right))
            best[rows, :] = jnp.maximum(best[rows, :], jnp.maximum(score[:, :128], score[:, 128:]))
        return 0

    lax.fori_loop(0, 6, correlate, 0)

    lane128 = lax.broadcasted_iota(jnp.int32, (256, 128), 1)
    row16 = lax.rem(lax.broadcasted_iota(jnp.int32, (256, 128), 0), 16)
    placed = jnp.zeros((256, 128), F32)
    for s in range(SURR):
        end = 2.0 * cos_phase[s : s + 1, FREQS - 1 : FREQS] * last
        energy = power * (2.0 / FRAMES) + end * end * (1.0 / FRAMES)
        top = jnp.max(best[pl.ds(s * 256, 256), :], axis=1, keepdims=True)
        top = top * lax.rsqrt(energy + EPS) * (math.sqrt(FRAMES) * 2.0 / FRAMES)
        placed = jnp.where(lane128 == row16 + 16 * s, top, placed)
    mine[...] = jnp.max(placed.reshape(16, 16, 128), axis=1)

    for d in range(1, 8):
        remote(mine, parts.at[k], part_send.at[d], part_recv.at[k], at_k(d)).start()
    parts[k] = mine[...]
    for d in range(1, 8):
        src = lax.rem(k + d, 8)
        remote(parts.at[src], parts.at[src], part_send.at[0], part_recv.at[src], at_k(1)).wait_recv()
    lane16 = lax.broadcasted_iota(jnp.int32, (16, 128), 1)
    row_lane = lax.broadcasted_iota(jnp.int32, (1, 128), 1)
    top_row = jnp.zeros((1, 128), F32)
    for s in range(SURR):
        full = jnp.zeros((16, 128), F32)
        for kk in range(8):
            place = (kk % 4) * 32 + (kk // 4) * 16
            moved = pltpu.roll(parts[kk], (place - 16 * s) % 128, 1)
            full = jnp.where((lane16 >= place) & (lane16 < place + 16), moved, full)
        out_tile[pl.ds(s * 16, 16), :] = full
        top_row = jnp.where(row_lane == s, jnp.max(jnp.max(full, axis=0, keepdims=True), axis=1, keepdims=True), top_row)

    own_top[...] = top_row
    for n, d in enumerate(NEAR):
        remote(own_top, top1.at[n], t1_send.at[n], t1_recv.at[n], at_z(d)).start()
    for n, d in enumerate(NEAR):
        remote(own_top, top1.at[n], t1_send.at[n], t1_recv.at[n], at_z(d)).wait_recv()
    value = jnp.maximum(top_row, jnp.max(top1[...], axis=0))
    wide_top[...] = value
    for n, d in enumerate((4, -4)):
        remote(wide_top, top2.at[n], t2_send.at[n], t2_recv.at[n], at_z(d)).start()
    for n, d in enumerate((4, -4)):
        remote(wide_top, top2.at[n], t2_send.at[n], t2_recv.at[n], at_z(d)).wait_recv()
    value = jnp.maximum(value, jnp.max(top2[...], axis=0))
    line_top[...] = value
    for d in range(1, 4):
        remote(line_top, top3.at[d - 1], t3_send.at[d - 1], t3_recv.at[d - 1], at_x(d)).start()
    for d in range(1, 4):
        remote(line_top, top3.at[d - 1], t3_send.at[d - 1], t3_recv.at[d - 1], at_x(d)).wait_recv()
    out_peak[...] = jnp.maximum(value, jnp.max(top3[...], axis=0))

    for h in range(2):
        target = h * 4 + z_low

        @pl.when(target != k)
        def _():
            remote(slab.at[pl.ds(h * 16, 16)], chunks.at[k], chunk_send.at[h], chunk_recv.at[k], (col, target)).wait_send()

    for d in range(1, 8):
        remote(phase, angles.at[k], ang_send.at[d], ang_recv.at[k], at_k(d)).wait_send()
        remote(mine, parts.at[k], part_send.at[d], part_recv.at[k], at_k(d)).wait_send()

    @pl.when(hub)
    def _():
        u = unit(0)
        for n, d in enumerate(NEAR):
            remote(held.at[u], held.at[u], near_send.at[n], unit_recv.at[u], at_z(d)).wait_send()
        u = unit(1)
        for n, d in enumerate((-3, -2, -1)):
            remote(held.at[u], held.at[u], relay_send.at[n], unit_recv.at[u], at_z(d)).wait_send()
        u = unit(-1)
        for n, d in enumerate((4, 3, 2, 1)):
            remote(held.at[u], held.at[u], relay_send.at[3 + n], unit_recv.at[u], at_z(d)).wait_send()

    for order, da in enumerate((0, 1, -1, 2)):
        u = unit(da)
        for n, d in enumerate((2, 1, 3)):
            remote(held.at[u], held.at[u], x_send.at[order * 3 + n], unit_recv.at[u], at_x(d)).wait_send()
    for n, d in enumerate(NEAR):
        remote(own_top, top1.at[n], t1_send.at[n], t1_recv.at[n], at_z(d)).wait_send()
    for n, d in enumerate((4, -4)):
        remote(wide_top, top2.at[n], t2_send.at[n], t2_recv.at[n], at_z(d)).wait_send()
    for d in range(1, 4):
        remote(line_top, top3.at[d - 1], t3_send.at[d - 1], t3_recv.at[d - 1], at_x(d)).wait_send()


def body(series, slab_series, phase_index, basis):
    dma = pltpu.SemaphoreType.DMA
    vmem = pl.BlockSpec(memory_space=pltpu.VMEM)
    hbm = pl.BlockSpec(memory_space=pl.ANY)
    tile, peak = pl.pallas_call(
        kernel,
        out_shape=(jax.ShapeDtypeStruct((64, 128), F32), jax.ShapeDtypeStruct((1, 128), F32)),
        in_specs=[hbm, vmem, vmem, hbm],
        out_specs=(vmem, vmem),
        scratch_shapes=[
            pltpu.VMEM((TP, COLS), BF16),
            pltpu.VMEM((4, FP, 128), F32),
            pltpu.VMEM((TP, TP), BF16),
            pltpu.VMEM((TP, TP), BF16),
            pltpu.VMEM((TP, COLS), BF16),
            pltpu.VMEM((16, 16, TP), BF16),
            pltpu.VMEM((8, 16, 150), F32),
            pltpu.VMEM((8, SURR, 75), jnp.int32),
            pltpu.VMEM((256, TP), F32),
            pltpu.VMEM((1024, TP), BF16),
            pltpu.VMEM((1024, 128), F32),
            pltpu.VMEM((16, 128), F32),
            pltpu.VMEM((8, 16, 128), F32),
            pltpu.VMEM((1, 128), F32),
            pltpu.VMEM((8, 1, 128), F32),
            pltpu.VMEM((1, 128), F32),
            pltpu.VMEM((2, 1, 128), F32),
            pltpu.VMEM((1, 128), F32),
            pltpu.VMEM((3, 1, 128), F32),
            dma, dma, dma((2,)), dma((8,)), dma((8,)), dma((8,)), dma((8,)), dma((7,)), dma((12,)), dma((16,)),
            dma((8,)), dma((8,)), dma((8,)), dma((8,)), dma((2,)), dma((2,)), dma((3,)), dma((3,)),
        ],
        compiler_params=pltpu.CompilerParams(
            collective_id=0, has_side_effects=True, vmem_limit_bytes=56 * 1024 * 1024
        ),
        name="surrogate_peaks",
    )(series, slab_series.T, phase_index, basis)
    return tile.reshape(SURR, 2048)[:, :, None], peak[0, :SURR]


def solution(mesh):
    basis = basis_tables()

    def run(series, slab_series, phase_index):
        placed = (P(None, "col"), P("tm", "col"), P(None, "tm"), P())
        step = jax.shard_map(
            body, mesh=mesh, in_specs=placed, out_specs=(P(None, None, "col"), P()), check_vma=False
        )
        return step(series, slab_series, phase_index, jnp.asarray(basis))

    return run
```

```python
import functools
import math

import jax
import jax.numpy as jnp
import numpy as np
from jax import lax
from jax.experimental import pallas as pl
from jax.experimental.pallas import tpu as pltpu
from jax.sharding import PartitionSpec as P

FRAMES = 1200
FREQS = 600
FP = 640
TP = 1280
SURR = 4
COLS = 1536
EPS = 1e-6
F32 = jnp.float32
BF16 = jnp.bfloat16
MESH = pl.DeviceIdType.MESH
NEAR = (4, -4, 3, -3, 2, -2, 1, -1)


def basis_tables():
    freq = np.arange(1, FP + 1)[:, None]
    lane = np.arange(128)[None, :]
    fine = 2.0 * np.pi * ((freq * lane) % FRAMES) / FRAMES
    step = np.broadcast_to(2.0 * np.pi * ((freq * 128) % FRAMES) / FRAMES, fine.shape)
    return np.stack([np.cos(fine), np.sin(fine), np.cos(step), np.sin(step)]).astype(np.float32)


def dot(a, b):
    return lax.dot_general(a, b, (((1,), (0,)), ((), ())), preferred_element_type=F32)


def dot_t(a, b):
    return lax.dot_general(a, b, (((1,), (1,)), ((), ())), preferred_element_type=F32)


def kernel(
    series, slab, phase, basis, out_tile, out_peak,
    cols, bas, thi, tlo, kc, held, chunks, angles, spec, rot, best, mine, parts, own_top, top1, wide_top, top2, tile,
    own_sem, col_sem, bas_sem, chunk_send, chunk_recv, ang_send, ang_recv, near_send, relay_send, x_send, unit_recv,
    kc_send, kc_recv, part_send, part_recv, t1_send, t1_recv, t2_send, t2_recv, tile_sem,
):
    col = lax.axis_index("col")
    k = lax.axis_index("tm")
    xx = lax.div(col, 16)
    z = lax.rem(col, 16)
    residue = lax.rem(k, 4)
    half = lax.div(k, 4)
    core = lax.rem(k, 2)
    z_low = lax.rem(z, 4)
    hub = z_low == residue

    def at_z(d):
        return (xx * 16 + lax.rem(z + d + 16, 16), k)

    def at_x(d):
        return (lax.rem(xx + d, 4) * 16 + z, k)

    def at_xz(dx, dz):
        return (lax.rem(xx + dx, 4) * 16 + lax.rem(z + dz + 16, 16), k)

    def at_k(d):
        return (col, lax.rem(k + d, 8))

    def remote(src, dst, send, recv, dev):
        return pltpu.make_async_remote_copy(
            src_ref=src, dst_ref=dst, send_sem=send, recv_sem=recv, device_id=dev, device_id_type=MESH
        )

    def behind_of(d):
        return lax.div(lax.rem(z + d - residue + 32, 16), 4)

    behind = behind_of(0)

    def unit_to_z(rel, d):
        here = rel * 4 + xx
        there = lax.rem(behind + rel - behind_of(d) + 8, 4) * 4 + xx
        return here, there

    series_copy = pltpu.make_async_copy(
        series.at[:, pl.ds(pl.multiple_of(core * 768, 256), 768)], cols.at[pl.ds(0, FRAMES)], col_sem
    )
    basis_copy = pltpu.make_async_copy(basis, bas, bas_sem)
    own_phase = pltpu.make_async_copy(phase, angles.at[k], own_sem.at[0])
    own_chunk = pltpu.make_async_copy(slab.at[pl.ds(pl.multiple_of(half * 16, 16), 16)], chunks.at[k], own_sem.at[1])

    barrier = pltpu.get_barrier_semaphore()
    peers = [at_k(d) for d in range(1, 8)] + [at_x(d) for d in range(1, 4)] + [at_z(d) for d in NEAR]
    for dev in peers:
        pl.semaphore_signal(barrier, inc=1, device_id=dev, device_id_type=MESH)

    own_phase.start()
    own_chunk.start()
    basis_copy.start()
    series_copy.start()

    def make_rows(i, _):
        at = pl.multiple_of(i * 64, 64)
        c = bas[0, pl.ds(at, 64), :]
        s = bas[1, pl.ds(at, 64), :]
        sc = bas[2, pl.ds(at, 64), :]
        ss = bas[3, pl.ds(at, 64), :]
        for a in range(10):
            lanes = pl.ds(a * 128, 128)
            for base, val in ((0, c), (FP, s)):
                hi = val.astype(BF16)
                thi[pl.ds(base + at, 64), lanes] = hi
                tlo[pl.ds(base + at, 64), lanes] = (val - hi.astype(F32)).astype(BF16)
            c, s = c * sc - s * ss, s * sc + c * ss
        return 0

    def norm_cols():
        def total(i, acc):
            x = cols[pl.ds(pl.multiple_of(i * 80, 16), 80), :].astype(F32)
            return acc + jnp.sum(x.reshape(10, 8, 768), axis=0)

        mean = jnp.sum(lax.fori_loop(0, 15, total, jnp.zeros((8, 768), F32)), axis=0, keepdims=True) * (1.0 / FRAMES)

        def squares(i, acc):
            x = cols[pl.ds(pl.multiple_of(i * 80, 16), 80), :].astype(F32) - mean
            return acc + jnp.sum((x * x).reshape(10, 8, 768), axis=0)

        scale = lax.rsqrt(jnp.sum(lax.fori_loop(0, 15, squares, jnp.zeros((8, 768), F32)), axis=0, keepdims=True) + EPS)

        def write(i, _):
            rows = pl.ds(pl.multiple_of(i * 80, 16), 80)
            cols[rows, :] = ((cols[rows, :].astype(F32) - mean) * scale).astype(BF16)
            return 0

        lax.fori_loop(0, 15, write, 0)

    def kc_copy(i):
        block = kc.at[core * 3 + i]
        return remote(block, block, kc_send.at[i], kc_recv.at[core * 3 + i], (col, k + 1 - 2 * core))

    def transform_cols(i):
        lanes = pl.ds(i * 256, 256)

        def block(b, _):
            rows = pl.ds(pl.multiple_of(b * 640, 128), 640)
            c = cols[:, lanes]
            kc[core * 3 + i, rows, :] = (dot(thi[rows, :], c) + dot(tlo[rows, :], c)).astype(BF16)
            return 0

        lax.fori_loop(0, 2, block, 0)
        kc_copy(i).start()

    pl.semaphore_wait(barrier, 18)

    for h in range(2):
        target = h * 4 + z_low

        @pl.when(target != k)
        def _():
            remote(slab.at[pl.ds(h * 16, 16)], chunks.at[k], chunk_send.at[h], chunk_recv.at[k], (col, target)).start()

    for d in range(1, 8):
        remote(phase, angles.at[k], ang_send.at[d], ang_recv.at[k], at_k(d)).start()

    own_chunk.wait()
    own_phase.wait()
    basis_copy.wait()
    lax.fori_loop(0, 10, make_rows, 0)

    @pl.when(hub)
    def _():
        for d in range(1, 8):
            src = lax.rem(k + d, 8)
            remote(chunks.at[src], chunks.at[src], chunk_send.at[0], chunk_recv.at[src], at_k(1)).wait_recv()
        x = jnp.concatenate([chunks[i] for i in range(8)], axis=1)
        x = x - jnp.sum(x, axis=1, keepdims=True) * (1.0 / FRAMES)
        held[xx] = jnp.concatenate([x, jnp.zeros((16, TP - FRAMES), F32)], axis=1).astype(BF16)
        for n, d in enumerate(NEAR):
            here, there = unit_to_z(0, d)
            remote(held.at[here], held.at[there], near_send.at[n], unit_recv.at[there], at_z(d)).start()

    def arrived(rel):
        here = rel * 4 + xx
        remote(held.at[here], held.at[here], near_send.at[0], unit_recv.at[here], at_z(1)).wait_recv()

    def relay_copies(rel):
        copies = []
        for n, d in enumerate((-3, -2, -1) if rel == 1 else (4, 3, 2, 1)):
            here, there = unit_to_z(rel, d)
            send = relay_send.at[n if rel == 1 else 3 + n]
            copies.append(remote(held.at[here], held.at[there], send, unit_recv.at[there], at_z(d)))
        return copies

    def x_copies(rel):
        here = rel * 4 + xx
        return [
            remote(held.at[here], held.at[here], x_send.at[rel * 3 + n], unit_recv.at[here], at_x(d))
            for n, d in enumerate((2, 1, 3))
        ]

    def relay(rel):
        @pl.when(hub)
        def _():
            for copy in relay_copies(rel):
                copy.start()

    def forward(rel):
        for copy in x_copies(rel):
            copy.start()

    cols[pl.ds(FRAMES, TP - FRAMES), :] = jnp.zeros((TP - FRAMES, 768), BF16)
    series_copy.wait()

    @pl.when(hub)
    def _():
        forward(0)

    norm_cols()
    transform_cols(0)

    @pl.when(jnp.logical_not(hub))
    def _():
        arrived(0)
        forward(0)

    arrived(1)
    relay(1)
    forward(1)

    @pl.when(hub)
    def _():
        arrived(3)

    relay(3)
    transform_cols(1)

    @pl.when(jnp.logical_not(hub))
    def _():
        arrived(3)

    forward(3)
    transform_cols(2)
    arrived(2)
    forward(2)

    for d in range(1, 8):
        src = lax.rem(k + d, 8)
        remote(angles.at[src], angles.at[src], ang_send.at[0], ang_recv.at[src], at_k(1)).wait_recv()
    turn = jnp.concatenate([angles[i] for i in range(8)] + [jnp.zeros((SURR, FP - FREQS), jnp.int32)], axis=1)
    angle = turn.astype(F32) * (2.0 * math.pi / FRAMES)
    lane = lax.broadcasted_iota(jnp.int32, (SURR, FP), 1)
    weight = jnp.where(lane < FREQS - 1, 1.0, jnp.where(lane == FREQS - 1, 0.5, 0.0)).astype(F32)
    cos_phase = jnp.cos(angle) * weight
    sin_phase = jnp.sin(angle) * weight
    lane1 = lax.broadcasted_iota(jnp.int32, (1, FP), 1)
    inner = (lane1 < FREQS - 1).astype(F32)
    lane128 = lax.broadcasted_iota(jnp.int32, (128, 128), 1)
    row16 = lax.rem(lax.broadcasted_iota(jnp.int32, (128, 128), 0), 16)

    def vertices(h):
        for rel in (2 * h, 2 * h + 1):
            for dx in range(1, 4):
                slot = rel * 4 + lax.rem(xx + dx, 4)
                remote(held.at[slot], held.at[slot], near_send.at[0], unit_recv.at[slot], at_x(dx)).wait_recv()
        xs = held[8 * h : 8 * h + 8].reshape(128, TP)
        for j in range(5):
            rows = pl.ds(j * 256, 256)
            spec[:, rows] = dot_t(xs, thi[rows, :]) + dot_t(xs, tlo[rows, :])
        sc = spec[:, 0:FP]
        ss = spec[:, FP:TP]
        power = jnp.sum((sc * sc + ss * ss) * inner, axis=1, keepdims=True)
        last = jnp.sum(jnp.where(lane1 == FREQS - 1, sc, 0.0), axis=1, keepdims=True)
        for s in range(SURR):
            cp = cos_phase[s : s + 1, :]
            sp = sin_phase[s : s + 1, :]
            rot[pl.ds(s * 128, 128), 0:FP] = (sc * cp + ss * sp).astype(BF16)
            rot[pl.ds(s * 128, 128), FP:TP] = (ss * cp - sc * sp).astype(BF16)
        best[...] = jnp.zeros_like(best)
        if h == 0:
            for i in range(3):
                block = kc.at[(1 - core) * 3 + i]
                remote(block, block, kc_send.at[i], kc_recv.at[(1 - core) * 3 + i], at_k(1)).wait_recv()

        def correlate(j, _):
            score = jnp.abs(dot(rot[...], kc[j]))
            best[...] = jnp.maximum(best[...], jnp.maximum(score[:, :128], score[:, 128:]))
            return 0

        lax.fori_loop(0, 6, correlate, 0)
        placed = jnp.zeros((128, 128), F32)
        for s in range(SURR):
            end = 2.0 * cos_phase[s : s + 1, FREQS - 1 : FREQS] * last
            energy = power * (2.0 / FRAMES) + end * end * (1.0 / FRAMES)
            top = jnp.max(best[pl.ds(s * 128, 128), :], axis=1, keepdims=True)
            top = top * lax.rsqrt(energy + EPS) * (math.sqrt(FRAMES) * 2.0 / FRAMES)
            placed = jnp.where(lane128 == row16 + 16 * s, top, placed)
        found = jnp.max(placed.reshape(8, 16, 128), axis=1)
        for n in range(8):
            row = (n % 4) * 4 + lax.rem(behind + 2 * h + n // 4, 4)
            mine[pl.ds(row, 1), :] = found[n : n + 1, :]

    vertices(0)
    vertices(1)

    for d in range(1, 8):
        remote(mine, parts.at[k], part_send.at[d], part_recv.at[k], at_k(d)).start()
    parts[k] = mine[...]
    for d in range(1, 8):
        src = lax.rem(k + d, 8)
        remote(parts.at[src], parts.at[src], part_send.at[0], part_recv.at[src], at_k(1)).wait_recv()

    own_top[...] = jnp.max(jnp.max(parts[...], axis=0), axis=0, keepdims=True)
    for n, d in enumerate(NEAR):
        remote(own_top, top1.at[n], t1_send.at[n], t1_recv.at[n], at_z(d)).start()
    lane16 = lax.broadcasted_iota(jnp.int32, (16, 128), 1)
    for s in range(SURR):
        full = jnp.zeros((16, 128), F32)
        for kk in range(8):
            place = (kk % 4) * 32 + (kk // 4) * 16
            moved = pltpu.roll(parts[kk], (place - 16 * s) % 128, 1)
            full = jnp.where((lane16 >= place) & (lane16 < place + 16), moved, full)
        tile[pl.ds(s * 16, 16), :] = full
    tile_copy = pltpu.make_async_copy(tile, out_tile, tile_sem)
    tile_copy.start()
    for n, d in enumerate(NEAR):
        remote(own_top, top1.at[n], t1_send.at[n], t1_recv.at[n], at_z(d)).wait_recv()
    wide_top[...] = jnp.maximum(own_top[...], jnp.max(top1[...], axis=0))
    across = [(dx, dz) for dz in (4, -4) for dx in (2, 1, 3, 0)]
    for n, (dx, dz) in enumerate(across):
        remote(wide_top, top2.at[n], t2_send.at[n], t2_recv.at[n], at_xz(dx, dz)).start()
    for n, (dx, dz) in enumerate(across):
        remote(wide_top, top2.at[n], t2_send.at[n], t2_recv.at[n], at_xz(dx, dz)).wait_recv()
    every = jnp.max(top2[...], axis=0)
    row_lane = lax.broadcasted_iota(jnp.int32, (1, 128), 1)
    result = jnp.zeros((1, 128), F32)
    for s in range(SURR):
        inside = (row_lane >= 16 * s) & (row_lane < 16 * s + 16)
        result = jnp.where(row_lane == s, jnp.max(jnp.where(inside, every, 0.0), axis=1, keepdims=True), result)
    out_peak[...] = result

    tile_copy.wait()
    for h in range(2):
        target = h * 4 + z_low

        @pl.when(target != k)
        def _():
            remote(slab.at[pl.ds(h * 16, 16)], chunks.at[k], chunk_send.at[h], chunk_recv.at[k], (col, target)).wait_send()

    for d in range(1, 8):
        remote(phase, angles.at[k], ang_send.at[d], ang_recv.at[k], at_k(d)).wait_send()
        remote(mine, parts.at[k], part_send.at[d], part_recv.at[k], at_k(d)).wait_send()

    @pl.when(hub)
    def _():
        for n, d in enumerate(NEAR):
            here, there = unit_to_z(0, d)
            remote(held.at[here], held.at[there], near_send.at[n], unit_recv.at[there], at_z(d)).wait_send()
        for copy in relay_copies(1) + relay_copies(3):
            copy.wait_send()

    for rel in range(4):
        for copy in x_copies(rel):
            copy.wait_send()
    for i in range(3):
        kc_copy(i).wait_send()
    for n, d in enumerate(NEAR):
        remote(own_top, top1.at[n], t1_send.at[n], t1_recv.at[n], at_z(d)).wait_send()
    for n, (dx, dz) in enumerate(across):
        remote(wide_top, top2.at[n], t2_send.at[n], t2_recv.at[n], at_xz(dx, dz)).wait_send()


def body(series, slab_series, phase_index, basis):
    dma = pltpu.SemaphoreType.DMA
    vmem = pl.BlockSpec(memory_space=pltpu.VMEM)
    hbm = pl.BlockSpec(memory_space=pl.ANY)
    tile, peak = pl.pallas_call(
        kernel,
        out_shape=(jax.ShapeDtypeStruct((64, 128), F32), jax.ShapeDtypeStruct((1, 128), F32)),
        in_specs=[hbm, hbm, hbm, hbm],
        out_specs=(hbm, vmem),
        scratch_shapes=[
            pltpu.VMEM((TP, 768), BF16),
            pltpu.VMEM((4, FP, 128), F32),
            pltpu.VMEM((TP, TP), BF16),
            pltpu.VMEM((TP, TP), BF16),
            pltpu.VMEM((6, TP, 256), BF16),
            pltpu.VMEM((16, 16, TP), BF16),
            pltpu.VMEM((8, 16, 150), F32),
            pltpu.VMEM((8, SURR, 75), jnp.int32),
            pltpu.VMEM((128, TP), F32),
            pltpu.VMEM((512, TP), BF16),
            pltpu.VMEM((512, 128), F32),
            pltpu.VMEM((16, 128), F32),
            pltpu.VMEM((8, 16, 128), F32),
            pltpu.VMEM((1, 128), F32),
            pltpu.VMEM((8, 1, 128), F32),
            pltpu.VMEM((1, 128), F32),
            pltpu.VMEM((8, 1, 128), F32),
            pltpu.VMEM((64, 128), F32),
            dma((2,)), dma, dma, dma((2,)), dma((8,)), dma((8,)), dma((8,)), dma((8,)), dma((7,)), dma((12,)), dma((16,)),
            dma((3,)), dma((6,)), dma((8,)), dma((8,)), dma((8,)), dma((8,)), dma((8,)), dma((8,)), dma,
        ],
        compiler_params=pltpu.CompilerParams(
            collective_id=0, has_side_effects=True, vmem_limit_bytes=56 * 1024 * 1024
        ),
        name="surrogate_peaks",
    )(series, slab_series.T, phase_index, basis)
    return tile.reshape(SURR, 2048)[:, :, None], peak[0, :SURR]


def solution(mesh):
    basis = basis_tables()

    def run(series, slab_series, phase_index):
        placed = (P(None, "col"), P("tm", "col"), P(None, "tm"), P())
        step = jax.shard_map(
            body, mesh=mesh, in_specs=placed, out_specs=(P(None, None, "col"), P()), check_vma=False
        )
        return step(series, slab_series, phase_index, jnp.asarray(basis))

    return run
```

```python
import functools
import math

import jax
import jax.numpy as jnp
import numpy as np
from jax import lax
from jax.experimental import pallas as pl
from jax.experimental.pallas import tpu as pltpu
from jax.sharding import PartitionSpec as P

FRAMES = 1200
FREQS = 600
FP = 640
TP = 1280
SURR = 4
COLS = 1536
EPS = 1e-6
F32 = jnp.float32
BF16 = jnp.bfloat16
MESH = pl.DeviceIdType.MESH
NEAR = (4, -4, 3, -3, 2, -2, 1, -1)
RING = (8, 7, -7, 6, -6, 5, -5, 4, -4, 3, -3, 2, -2, 1, -1)
PLANE = tuple((dx, dk) for dx in (2, 1, 3, 0) for dk in (4, 5, 3, 2, 6, 7, 1, 0) if (dx, dk) != (0, 0))


def basis_tables():
    freq = np.arange(1, FP + 1)[:, None]
    lane = np.arange(128)[None, :]
    fine = 2.0 * np.pi * ((freq * lane) % FRAMES) / FRAMES
    step = np.broadcast_to(2.0 * np.pi * ((freq * 128) % FRAMES) / FRAMES, fine.shape)
    return np.stack([np.cos(fine), np.sin(fine), np.cos(step), np.sin(step)]).astype(np.float32)


def dot(a, b):
    return lax.dot_general(a, b, (((1,), (0,)), ((), ())), preferred_element_type=F32)


def dot_t(a, b):
    return lax.dot_general(a, b, (((1,), (1,)), ((), ())), preferred_element_type=F32)


def kernel(
    series, slab, phase, basis, out_tile, out_peak,
    cols, bas, thi, tlo, kc, held, chunks, angles, spec, rot, best, mine, parts, own_top, top1, wide_top, top2,
    own_sem, col_sem, bas_sem, chunk_send, chunk_recv, ang_send, ang_recv, near_send, relay_send, x_send, unit_recv,
    kc_send, kc_recv, part_send, part_recv, t1_send, t1_recv, t2_send, t2_recv, hello,
):
    col = lax.axis_index("col")
    k = lax.axis_index("tm")
    xx = lax.div(col, 16)
    z = lax.rem(col, 16)
    residue = lax.rem(k, 4)
    half = lax.div(k, 4)
    core = lax.rem(k, 2)
    z_low = lax.rem(z, 4)
    hub = z_low == residue

    def at_z(d):
        return (xx * 16 + lax.rem(z + d + 16, 16), k)

    def at_x(d):
        return (lax.rem(xx + d, 4) * 16 + z, k)

    def at_xk(dx, dk):
        return (lax.rem(xx + dx, 4) * 16 + z, lax.rem(k + dk, 8))

    def at_k(d):
        return (col, lax.rem(k + d, 8))

    def remote(src, dst, send, recv, dev):
        return pltpu.make_async_remote_copy(
            src_ref=src, dst_ref=dst, send_sem=send, recv_sem=recv, device_id=dev, device_id_type=MESH
        )

    def await_sent(ref, sem):
        remote(ref, ref, sem, sem, at_k(1)).wait_send()

    def await_all(ref, sem):
        remote(ref, ref, sem, sem, at_k(1)).wait_recv()

    def behind_of(d):
        return lax.div(lax.rem(z + d - residue + 32, 16), 4)

    behind = behind_of(0)

    def unit_to_z(rel, d):
        here = rel * 4 + xx
        there = lax.rem(behind + rel - behind_of(d) + 8, 4) * 4 + xx
        return here, there

    series_copy = pltpu.make_async_copy(
        series.at[:, pl.ds(pl.multiple_of(core * 768, 256), 768)], cols.at[pl.ds(0, FRAMES)], col_sem
    )
    basis_copy = pltpu.make_async_copy(basis, bas, bas_sem)
    own_phase = pltpu.make_async_copy(phase, angles.at[k], own_sem.at[0])
    own_chunk = pltpu.make_async_copy(slab.at[pl.ds(pl.multiple_of(half * 16, 16), 16)], chunks.at[k], own_sem.at[1])

    barrier = pltpu.get_barrier_semaphore()
    peers = [at_k(d) for d in range(1, 8)] + [at_x(d) for d in range(1, 4)] + [at_z(d) for d in (2, -2, 1, -1)]
    for dev in peers:
        pl.semaphore_signal(barrier, inc=1, device_id=dev, device_id_type=MESH)

    own_phase.start()
    own_chunk.start()
    basis_copy.start()
    series_copy.start()

    def make_rows(i, _):
        at = pl.multiple_of(i * 64, 64)
        c = bas[0, pl.ds(at, 64), :]
        s = bas[1, pl.ds(at, 64), :]
        sc = bas[2, pl.ds(at, 64), :]
        ss = bas[3, pl.ds(at, 64), :]
        for a in range(10):
            lanes = pl.ds(a * 128, 128)
            for base, val in ((0, c), (FP, s)):
                hi = val.astype(BF16)
                thi[pl.ds(base + at, 64), lanes] = hi
                tlo[pl.ds(base + at, 64), lanes] = (val - hi.astype(F32)).astype(BF16)
            c, s = c * sc - s * ss, s * sc + c * ss
        return 0

    def norm_cols():
        def total(i, acc):
            x = cols[pl.ds(pl.multiple_of(i * 80, 16), 80), :].astype(F32)
            return acc + jnp.sum(x.reshape(10, 8, 768), axis=0)

        mean = jnp.sum(lax.fori_loop(0, 15, total, jnp.zeros((8, 768), F32)), axis=0, keepdims=True) * (1.0 / FRAMES)

        def squares(i, acc):
            x = cols[pl.ds(pl.multiple_of(i * 80, 16), 80), :].astype(F32) - mean
            return acc + jnp.sum((x * x).reshape(10, 8, 768), axis=0)

        scale = lax.rsqrt(jnp.sum(lax.fori_loop(0, 15, squares, jnp.zeros((8, 768), F32)), axis=0, keepdims=True) + EPS)

        def write(i, _):
            rows = pl.ds(pl.multiple_of(i * 80, 16), 80)
            cols[rows, :] = ((cols[rows, :].astype(F32) - mean) * scale).astype(BF16)
            return 0

        lax.fori_loop(0, 15, write, 0)

    def kc_copy(i):
        block = kc.at[core * 3 + i]
        return remote(block, block, kc_send, kc_recv, (col, k + 1 - 2 * core))

    def transform_cols(i):
        lanes = pl.ds(i * 256, 256)

        def block(b, _):
            rows = pl.ds(pl.multiple_of(b * 640, 128), 640)
            c = cols[:, lanes]
            kc[core * 3 + i, rows, :] = (dot(thi[rows, :], c) + dot(tlo[rows, :], c)).astype(BF16)
            return 0

        lax.fori_loop(0, 2, block, 0)
        kc_copy(i).start()

    pl.semaphore_wait(barrier, 14)

    for h in range(2):
        target = h * 4 + z_low

        @pl.when(target != k)
        def _():
            remote(slab.at[pl.ds(h * 16, 16)], chunks.at[k], chunk_send.at[h], chunk_recv, (col, target)).start()

    for d in (2, -2):
        pl.semaphore_signal(hello, inc=1, device_id=at_z(d), device_id_type=MESH)
    for d in range(1, 8):
        remote(phase, angles.at[k], ang_send, ang_recv, at_k(d)).start()

    basis_copy.wait()
    lax.fori_loop(0, 10, make_rows, 0)
    own_chunk.wait()
    own_phase.wait()
    pl.semaphore_wait(hello, 2)

    @pl.when(hub)
    def _():
        await_all(chunks.at[pl.ds(0, 7)], chunk_recv)
        x = jnp.concatenate([chunks[i] for i in range(8)], axis=1)
        x = x - jnp.sum(x, axis=1, keepdims=True) * (1.0 / FRAMES)
        held[xx] = jnp.concatenate([x, jnp.zeros((16, TP - FRAMES), F32)], axis=1).astype(BF16)
        for n, d in enumerate(NEAR):
            here, there = unit_to_z(0, d)
            remote(held.at[here], held.at[there], near_send, unit_recv.at[there], at_z(d)).start()

    def arrived(rel):
        here = rel * 4 + xx
        remote(held.at[here], held.at[here], near_send, unit_recv.at[here], at_z(1)).wait_recv()

    def relay_copies(rel):
        copies = []
        for d in (-3, -2, -1) if rel == 1 else (4, 3, 2, 1):
            here, there = unit_to_z(rel, d)
            copies.append(remote(held.at[here], held.at[there], relay_send, unit_recv.at[there], at_z(d)))
        return copies

    def x_copies(rel):
        here = rel * 4 + xx
        return [
            remote(held.at[here], held.at[here], x_send, unit_recv.at[here], at_x(d))
            for d in (2, 1, 3)
        ]

    def relay(rel):
        for copy in relay_copies(rel):
            copy.start()

    def forward(rel):
        for copy in x_copies(rel):
            copy.start()

    @pl.when(hub)
    def _():
        forward(0)

    cols[pl.ds(FRAMES, TP - FRAMES), :] = jnp.zeros((TP - FRAMES, 768), BF16)
    series_copy.wait()
    norm_cols()

    turned = lax.rem(lax.div(behind + 1, 2), 2)

    def neighbour(rel):
        arrived(rel)
        relay(rel)
        forward(rel)

    transform_cols(0)

    @pl.when(jnp.logical_not(hub))
    def _():
        arrived(0)
        forward(0)

    @pl.when(hub & (turned == 0))
    def _():
        neighbour(1)

    @pl.when(hub & (turned == 1))
    def _():
        neighbour(3)

    transform_cols(1)

    @pl.when(hub & (turned == 0))
    def _():
        neighbour(3)

    @pl.when(hub & (turned == 1))
    def _():
        neighbour(1)

    @pl.when(jnp.logical_not(hub))
    def _():
        arrived(1)
        forward(1)

    transform_cols(2)

    @pl.when(jnp.logical_not(hub))
    def _():
        arrived(3)
        forward(3)

    arrived(2)
    forward(2)

    await_all(angles.at[pl.ds(0, 7)], ang_recv)
    turn = jnp.concatenate([angles[i] for i in range(8)] + [jnp.zeros((SURR, FP - FREQS), jnp.int32)], axis=1)
    angle = turn.astype(F32) * (2.0 * math.pi / FRAMES)
    lane = lax.broadcasted_iota(jnp.int32, (SURR, FP), 1)
    weight = jnp.where(lane < FREQS - 1, 1.0, jnp.where(lane == FREQS - 1, 0.5, 0.0)).astype(F32)
    cos_phase = jnp.cos(angle) * weight
    sin_phase = jnp.sin(angle) * weight
    lane1 = lax.broadcasted_iota(jnp.int32, (1, FP), 1)
    inner = (lane1 < FREQS - 1).astype(F32)
    lane128 = lax.broadcasted_iota(jnp.int32, (256, 128), 1)
    row16 = lax.rem(lax.broadcasted_iota(jnp.int32, (256, 128), 0), 16)

    def spectra(h):
        for rel in ((0, 1), (3, 2))[h]:
            for dx in range(1, 4):
                slot = rel * 4 + lax.rem(xx + dx, 4)
                await_all(held.at[slot], unit_recv.at[slot])
        xs = held[8 * h : 8 * h + 8].reshape(128, TP)
        for j in range(5):
            rows = pl.ds(j * 256, 256)
            spec[pl.ds(128 * h, 128), rows] = dot_t(xs, thi[rows, :]) + dot_t(xs, tlo[rows, :])

    def rotate(h, s):
        sc = spec[pl.ds(128 * h, 128), 0:FP]
        ss = spec[pl.ds(128 * h, 128), FP:TP]
        cp = cos_phase[s : s + 1, :]
        sp = sin_phase[s : s + 1, :]
        rows = pl.ds(s * 256 + 128 * h, 128)
        rot[rows, 0:FP] = (sc * cp + ss * sp).astype(BF16)
        rot[rows, FP:TP] = (ss * cp - sc * sp).astype(BF16)

    spectra(0)
    for s in range(SURR):
        rotate(0, s)
    await_all(kc.at[pl.ds(0, 3)], kc_recv)
    spectra(1)
    for s in range(SURR):
        rotate(1, s)
        rows = pl.ds(s * 256, 256)
        for j in range(6):
            score = jnp.abs(dot(rot[rows, :], kc[j]))
            score = jnp.maximum(score[:, :128], score[:, 128:])
            best[rows, :] = score if j == 0 else jnp.maximum(best[rows, :], score)
    sc = spec[:, 0:FP]
    ss = spec[:, FP:TP]
    power = jnp.sum((sc * sc + ss * ss) * inner, axis=1, keepdims=True)
    last = jnp.sum(jnp.where(lane1 == FREQS - 1, sc, 0.0), axis=1, keepdims=True)
    placed = jnp.zeros((256, 128), F32)
    for s in range(SURR):
        end = 2.0 * cos_phase[s : s + 1, FREQS - 1 : FREQS] * last
        energy = power * (2.0 / FRAMES) + end * end * (1.0 / FRAMES)
        top = jnp.max(best[pl.ds(s * 256, 256), :], axis=1, keepdims=True)
        top = top * lax.rsqrt(energy + EPS) * (math.sqrt(FRAMES) * 2.0 / FRAMES)
        placed = jnp.where(lane128 == row16 + 16 * s, top, placed)
    found = jnp.max(placed.reshape(16, 16, 128), axis=1)
    for n in range(16):
        row = (n % 4) * 4 + lax.rem(behind + n // 4, 4)
        mine[pl.ds(row, 1), :] = found[n : n + 1, :]

    own_top[...] = jnp.max(mine[...], axis=0, keepdims=True)
    for n, (dx, dk) in enumerate(PLANE):
        remote(own_top, top1.at[n], t1_send, t1_recv, at_xk(dx, dk)).start()
    for d in range(1, 8):
        remote(mine, parts.at[k], part_send, part_recv, at_k(d)).start()
    parts[k] = mine[...]
    await_all(top1, t1_recv)
    wide_top[...] = jnp.maximum(own_top[...], jnp.max(top1[...], axis=0))
    for n, d in enumerate(RING):
        remote(wide_top, top2.at[n], t2_send, t2_recv, at_z(d)).start()
    await_all(parts.at[pl.ds(0, 7)], part_recv)
    lane16 = lax.broadcasted_iota(jnp.int32, (16, 128), 1)
    for s in range(SURR):
        full = jnp.zeros((16, 128), F32)
        for kk in range(8):
            place = (kk % 4) * 32 + (kk // 4) * 16
            moved = pltpu.roll(parts[kk], (place - 16 * s) % 128, 1)
            full = jnp.where((lane16 >= place) & (lane16 < place + 16), moved, full)
        out_tile[pl.ds(s * 16, 16), :] = full
    await_all(top2, t2_recv)
    every = jnp.maximum(wide_top[...], jnp.max(top2[...], axis=0))
    row_lane = lax.broadcasted_iota(jnp.int32, (1, 128), 1)
    result = jnp.zeros((1, 128), F32)
    for s in range(SURR):
        inside = (row_lane >= 16 * s) & (row_lane < 16 * s + 16)
        result = jnp.where(row_lane == s, jnp.max(jnp.where(inside, every, 0.0), axis=1, keepdims=True), result)
    out_peak[...] = result

    for h in range(2):
        target = h * 4 + z_low

        @pl.when(target != k)
        def _():
            remote(slab.at[pl.ds(h * 16, 16)], chunks.at[k], chunk_send.at[h], chunk_recv, (col, target)).wait_send()

    @pl.when(hub)
    def _():
        await_sent(held.at[pl.ds(0, 8)], near_send)
        await_sent(held.at[pl.ds(0, 7)], relay_send)

    await_sent(angles.at[pl.ds(0, 7)], ang_send)
    await_sent(held.at[pl.ds(0, 12)], x_send)
    await_sent(kc.at[pl.ds(0, 3)], kc_send)
    await_sent(parts.at[pl.ds(0, 7)], part_send)
    await_sent(top1, t1_send)
    await_sent(top2, t2_send)


def body(series, slab_series, phase_index, basis):
    dma = pltpu.SemaphoreType.DMA
    vmem = pl.BlockSpec(memory_space=pltpu.VMEM)
    hbm = pl.BlockSpec(memory_space=pl.ANY)
    tile, peak = pl.pallas_call(
        kernel,
        out_shape=(pltpu.VMEM((64, 128), F32), pltpu.VMEM((1, 128), F32)),
        in_specs=[hbm, hbm, hbm, hbm],
        out_specs=(vmem, vmem),
        scratch_shapes=[
            pltpu.VMEM((TP, 768), BF16),
            pltpu.VMEM((4, FP, 128), F32),
            pltpu.VMEM((TP, TP), BF16),
            pltpu.VMEM((TP, TP), BF16),
            pltpu.VMEM((6, TP, 256), BF16),
            pltpu.VMEM((16, 16, TP), BF16),
            pltpu.VMEM((8, 16, 150), F32),
            pltpu.VMEM((8, SURR, 75), jnp.int32),
            pltpu.VMEM((256, TP), F32),
            pltpu.VMEM((1024, TP), BF16),
            pltpu.VMEM((1024, 128), F32),
            pltpu.VMEM((16, 128), F32),
            pltpu.VMEM((8, 16, 128), F32),
            pltpu.VMEM((1, 128), F32),
            pltpu.VMEM((31, 1, 128), F32),
            pltpu.VMEM((1, 128), F32),
            pltpu.VMEM((15, 1, 128), F32),
            dma((2,)), dma, dma, dma((2,)), dma, dma, dma, dma, dma, dma, dma((16,)),
            dma, dma, dma, dma, dma, dma, dma, dma, pltpu.SemaphoreType.REGULAR,
        ],
        compiler_params=pltpu.CompilerParams(
            collective_id=0, has_side_effects=True, vmem_limit_bytes=56 * 1024 * 1024
        ),
        name="surrogate_peaks",
    )(series, slab_series.T, phase_index, basis)
    return tile.reshape(SURR, 2048)[:, :, None], peak[0, :SURR]


def solution(mesh):
    basis = basis_tables()

    def run(series, slab_series, phase_index):
        placed = (P(None, "col"), P("tm", "col"), P(None, "tm"), P())
        step = jax.shard_map(
            body, mesh=mesh, in_specs=placed, out_specs=(P(None, None, "col"), P()), check_vma=False
        )
        return step(series, slab_series, phase_index, jnp.asarray(basis))

    return run
```

```python
import functools
import math

import jax
import jax.numpy as jnp
import numpy as np
from jax import lax
from jax.experimental import pallas as pl
from jax.experimental.pallas import tpu as pltpu
from jax.sharding import PartitionSpec as P

FRAMES = 1200
FREQS = 600
FP = 640
TP = 1280
SURR = 4
COLS = 1536
EPS = 1e-6
F32 = jnp.float32
BF16 = jnp.bfloat16
MESH = pl.DeviceIdType.MESH
NEAR = (4, -4, 3, -3, 2, -2, 1, -1)
RING = (8, 7, -7, 6, -6, 5, -5, 4, -4, 3, -3, 2, -2, 1, -1)
PLANE = tuple((dx, dk) for dx in (2, 1, 3, 0) for dk in (4, 5, 3, 2, 6, 7, 1, 0) if (dx, dk) != (0, 0))


def basis_tables():
    freq = np.arange(1, FP + 1)[:, None]
    lane = np.arange(128)[None, :]
    fine = 2.0 * np.pi * ((freq * lane) % FRAMES) / FRAMES
    step = np.broadcast_to(2.0 * np.pi * ((freq * 128) % FRAMES) / FRAMES, fine.shape)
    return np.stack([np.cos(fine), np.sin(fine), np.cos(step), np.sin(step)]).astype(np.float32)


def dot(a, b):
    return lax.dot_general(a, b, (((1,), (0,)), ((), ())), preferred_element_type=F32)


def dot_t(a, b):
    return lax.dot_general(a, b, (((1,), (1,)), ((), ())), preferred_element_type=F32)


def kernel(
    series, slab, phase, basis, out_tile, out_peak,
    cols, bas, thi, tlo, kc, held, block_rows, chunks, angles, spec, rot, best, mine, parts, own_top, top1, wide_top, top2,
    own_sem, col_sem, bas_sem, chunk_send, chunk_recv, ang_send, ang_recv, near_send, relay_send, x_send, x_recv, unit_recv,
    kc_send, kc_recv, part_send, part_recv, t1_send, t1_recv, t2_send, t2_recv, hello,
):
    col = lax.axis_index("col")
    k = lax.axis_index("tm")
    xx = lax.div(col, 16)
    z = lax.rem(col, 16)
    residue = lax.rem(k, 2) * 2 + lax.div(lax.rem(k, 4), 2)
    half = lax.div(k, 4)
    core = lax.rem(k, 2)
    z_low = lax.rem(z, 4)
    hub = z_low == residue

    def at_z(d):
        return (xx * 16 + lax.rem(z + d + 16, 16), k)

    def at_x(d):
        return (lax.rem(xx + d, 4) * 16 + z, k)

    def at_xk(dx, dk):
        return (lax.rem(xx + dx, 4) * 16 + z, lax.rem(k + dk, 8))

    def at_k(d):
        return (col, lax.rem(k + d, 8))

    def remote(src, dst, send, recv, dev):
        return pltpu.make_async_remote_copy(
            src_ref=src, dst_ref=dst, send_sem=send, recv_sem=recv, device_id=dev, device_id_type=MESH
        )

    def await_sent(ref, sem):
        remote(ref, ref, sem, sem, at_k(1)).wait_send()

    def await_all(ref, sem):
        remote(ref, ref, sem, sem, at_k(1)).wait_recv()

    def behind_of(d):
        return lax.div(lax.rem(z + d - residue + 32, 16), 4)

    behind = behind_of(0)

    def unit_to_z(rel, d):
        here = rel * 4 + xx
        there = lax.rem(behind + rel - behind_of(d) + 8, 4) * 4 + xx
        return here, there

    series_copy = pltpu.make_async_copy(
        series.at[:, pl.ds(pl.multiple_of(core * 768, 256), 768)], cols.at[pl.ds(0, FRAMES)], col_sem
    )
    basis_copy = pltpu.make_async_copy(basis, bas, bas_sem)
    own_phase = pltpu.make_async_copy(phase, angles.at[k], own_sem.at[0])
    own_chunk = pltpu.make_async_copy(slab, block_rows, own_sem.at[1])

    barrier = pltpu.get_barrier_semaphore()
    peers = [at_k(d) for d in range(1, 8)] + [at_x(d) for d in range(1, 4)] + [at_z(d) for d in (2, -2, 1, -1)]
    for dev in peers:
        pl.semaphore_signal(barrier, inc=1, device_id=dev, device_id_type=MESH)

    own_phase.start()
    own_chunk.start()
    basis_copy.start()
    series_copy.start()

    def make_rows(i, _):
        at = pl.multiple_of(i * 64, 64)
        c = bas[0, pl.ds(at, 64), :]
        s = bas[1, pl.ds(at, 64), :]
        sc = bas[2, pl.ds(at, 64), :]
        ss = bas[3, pl.ds(at, 64), :]
        for a in range(10):
            lanes = pl.ds(a * 128, 128)
            for base, val in ((0, c), (FP, s)):
                hi = val.astype(BF16)
                thi[pl.ds(base + at, 64), lanes] = hi
                tlo[pl.ds(base + at, 64), lanes] = (val - hi.astype(F32)).astype(BF16)
            c, s = c * sc - s * ss, s * sc + c * ss
        return 0

    def norm_cols():
        def total(i, acc):
            x = cols[pl.ds(pl.multiple_of(i * 80, 16), 80), :].astype(F32)
            return acc + jnp.sum(x.reshape(10, 8, 768), axis=0)

        mean = jnp.sum(lax.fori_loop(0, 15, total, jnp.zeros((8, 768), F32)), axis=0, keepdims=True) * (1.0 / FRAMES)

        def squares(i, acc):
            x = cols[pl.ds(pl.multiple_of(i * 80, 16), 80), :].astype(F32) - mean
            return acc + jnp.sum((x * x).reshape(10, 8, 768), axis=0)

        scale = lax.rsqrt(jnp.sum(lax.fori_loop(0, 15, squares, jnp.zeros((8, 768), F32)), axis=0, keepdims=True) + EPS)

        def write(i, _):
            rows = pl.ds(pl.multiple_of(i * 80, 16), 80)
            cols[rows, :] = ((cols[rows, :].astype(F32) - mean) * scale).astype(BF16)
            return 0

        lax.fori_loop(0, 15, write, 0)

    def kc_copy(i):
        block = kc.at[core * 3 + i]
        return remote(block, block, kc_send, kc_recv, (col, k + 1 - 2 * core))

    def transform_cols(i):
        lanes = pl.ds(i * 256, 256)

        def block(b, _):
            rows = pl.ds(pl.multiple_of(b * 640, 128), 640)
            c = cols[:, lanes]
            kc[core * 3 + i, rows, :] = (dot(thi[rows, :], c) + dot(tlo[rows, :], c)).astype(BF16)
            return 0

        lax.fori_loop(0, 2, block, 0)
        kc_copy(i).start()

    own_chunk.wait()
    pl.semaphore_wait(barrier, 14)

    for h in range(2):
        target = h * 4 + lax.rem(z_low, 2) * 2 + lax.div(z_low, 2)

        @pl.when(target != k)
        def _():
            remote(block_rows.at[pl.ds(h * 16, 16)], chunks.at[k], chunk_send.at[h], chunk_recv, (col, target)).start()

    for d in (2, -2):
        pl.semaphore_signal(hello, inc=1, device_id=at_z(d), device_id_type=MESH)
    for d in range(1, 8):
        remote(phase, angles.at[k], ang_send, ang_recv, at_k(d)).start()

    basis_copy.wait()
    lax.fori_loop(0, 10, make_rows, 0)
    own_phase.wait()
    pl.semaphore_wait(hello, 2)

    def send_own(hops):
        for d in hops:
            here, there = unit_to_z(0, d)
            remote(held.at[here], held.at[there], near_send, unit_recv.at[lax.div(there, 4)], at_z(d)).start()

    @pl.when(hub)
    def _():
        chunks[k] = block_rows[pl.ds(pl.multiple_of(half * 16, 16), 16), :]
        await_all(chunks.at[pl.ds(0, 7)], chunk_recv)
        x = jnp.concatenate([chunks[i] for i in range(8)], axis=1)
        x = x - jnp.sum(x, axis=1, keepdims=True) * (1.0 / FRAMES)
        held[xx] = jnp.concatenate([x, jnp.zeros((16, TP - FRAMES), F32)], axis=1).astype(BF16)
        send_own(NEAR)

    def arrived(rel):
        here = rel * 4 + xx
        remote(held.at[here], held.at[here], near_send, unit_recv.at[rel], at_z(1)).wait_recv()

    def relay_copies(rel):
        copies = []
        for d in (-3, -2, -1) if rel == 1 else (4, 3, 2, 1):
            here, there = unit_to_z(rel, d)
            copies.append(remote(held.at[here], held.at[there], relay_send, unit_recv.at[lax.div(there, 4)], at_z(d)))
        return copies

    def x_copies(rel, hops=(2, 1, 3)):
        here = rel * 4 + xx
        return [remote(held.at[here], held.at[here], x_send, x_recv.at[rel // 2], at_x(d)) for d in hops]

    def relay(rel):
        for copy in relay_copies(rel):
            copy.start()

    def forward(rel):
        for copy in x_copies(rel):
            copy.start()

    @pl.when(hub)
    def _():
        forward(0)

    cols[pl.ds(FRAMES, TP - FRAMES), :] = jnp.zeros((TP - FRAMES, 768), BF16)
    series_copy.wait()
    norm_cols()

    turned = lax.rem(lax.div(behind + 1, 2), 2)

    def neighbour(rel):
        arrived(rel)
        relay(rel)
        forward(rel)

    transform_cols(0)

    @pl.when(jnp.logical_not(hub))
    def _():
        arrived(0)
        forward(0)

    @pl.when(hub & (turned == 0))
    def _():
        neighbour(1)
        neighbour(3)

    @pl.when(hub & (turned == 1))
    def _():
        neighbour(3)
        neighbour(1)

    transform_cols(1)

    @pl.when(jnp.logical_not(hub))
    def _():
        arrived(1)
        forward(1)

    transform_cols(2)

    @pl.when(jnp.logical_not(hub))
    def _():
        arrived(3)
        x_copies(3, (2,))[0].start()
        arrived(2)
        x_copies(2, (2,))[0].start()
        for rel in (3, 2):
            for copy in x_copies(rel, (1, 3)):
                copy.start()

    @pl.when(hub)
    def _():
        arrived(2)
        forward(2)

    await_all(angles.at[pl.ds(0, 7)], ang_recv)
    turn = jnp.concatenate([angles[i] for i in range(8)] + [jnp.zeros((SURR, FP - FREQS), jnp.int32)], axis=1)
    angle = turn.astype(F32) * (2.0 * math.pi / FRAMES)
    lane = lax.broadcasted_iota(jnp.int32, (SURR, FP), 1)
    weight = jnp.where(lane < FREQS - 1, 1.0, jnp.where(lane == FREQS - 1, 0.5, 0.0)).astype(F32)
    cos_phase = jnp.cos(angle) * weight
    sin_phase = jnp.sin(angle) * weight
    lane1 = lax.broadcasted_iota(jnp.int32, (1, FP), 1)
    inner = (lane1 < FREQS - 1).astype(F32)
    lane128 = lax.broadcasted_iota(jnp.int32, (256, 128), 1)
    row16 = lax.rem(lax.broadcasted_iota(jnp.int32, (256, 128), 0), 16)

    def spectra(h):
        await_all(held.at[pl.ds(0, 6)], x_recv.at[h])
        xs = held[8 * h : 8 * h + 8].reshape(128, TP)
        for j in range(5):
            rows = pl.ds(j * 256, 256)
            spec[pl.ds(128 * h, 128), rows] = dot_t(xs, thi[rows, :]) + dot_t(xs, tlo[rows, :])

    def rotate(h, s):
        sc = spec[pl.ds(128 * h, 128), 0:FP]
        ss = spec[pl.ds(128 * h, 128), FP:TP]
        cp = cos_phase[s : s + 1, :]
        sp = sin_phase[s : s + 1, :]
        rows = pl.ds(s * 256 + 128 * h, 128)
        rot[rows, 0:FP] = (sc * cp + ss * sp).astype(BF16)
        rot[rows, FP:TP] = (ss * cp - sc * sp).astype(BF16)

    spectra(0)
    for s in range(SURR):
        rotate(0, s)
    await_all(kc.at[pl.ds(0, 3)], kc_recv)
    spectra(1)
    sc = spec[:, 0:FP]
    ss = spec[:, FP:TP]
    power = jnp.sum((sc * sc + ss * ss) * inner, axis=1, keepdims=True)
    last = jnp.sum(jnp.where(lane1 == FREQS - 1, sc, 0.0), axis=1, keepdims=True)
    scales = []
    for s in range(SURR):
        end = 2.0 * cos_phase[s : s + 1, FREQS - 1 : FREQS] * last
        energy = power * (2.0 / FRAMES) + end * end * (1.0 / FRAMES)
        scales.append(lax.rsqrt(energy + EPS) * (math.sqrt(FRAMES) * 2.0 / FRAMES))
    for s in range(SURR):
        rotate(1, s)
        rows = pl.ds(s * 256, 256)
        for j in range(6):
            score = jnp.abs(dot(rot[rows, :], kc[j]))
            score = jnp.maximum(score[:, :128], score[:, 128:])
            best[rows, :] = score if j == 0 else jnp.maximum(best[rows, :], score)
    placed = jnp.zeros((256, 128), F32)
    for s in range(SURR):
        top = jnp.max(best[pl.ds(s * 256, 256), :], axis=1, keepdims=True) * scales[s]
        placed = jnp.where(lane128 == row16 + 16 * s, top, placed)
    found = jnp.max(placed.reshape(16, 16, 128), axis=1)
    for n in range(16):
        row = (n % 4) * 4 + lax.rem(behind + n // 4, 4)
        mine[pl.ds(row, 1), :] = found[n : n + 1, :]

    own_top[...] = jnp.max(mine[...], axis=0, keepdims=True)
    for n, (dx, dk) in enumerate(PLANE):
        remote(own_top, top1.at[n], t1_send, t1_recv, at_xk(dx, dk)).start()
    for d in range(1, 8):
        remote(mine, parts.at[k], part_send, part_recv, at_k(d)).start()
    parts[k] = mine[...]
    await_all(top1, t1_recv)
    wide_top[...] = jnp.maximum(own_top[...], jnp.max(top1[...], axis=0))
    for n, d in enumerate(RING):
        remote(wide_top, top2.at[n], t2_send, t2_recv, at_z(d)).start()
    await_all(parts.at[pl.ds(0, 7)], part_recv)
    lane16 = lax.broadcasted_iota(jnp.int32, (16, 128), 1)
    for s in range(SURR):
        full = jnp.zeros((16, 128), F32)
        for kk in range(8):
            place = (kk % 2 * 2 + kk % 4 // 2) * 32 + (kk // 4) * 16
            moved = pltpu.roll(parts[kk], (place - 16 * s) % 128, 1)
            full = jnp.where((lane16 >= place) & (lane16 < place + 16), moved, full)
        out_tile[pl.ds(s * 16, 16), :] = full
    await_all(top2, t2_recv)
    every = jnp.maximum(wide_top[...], jnp.max(top2[...], axis=0))
    row_lane = lax.broadcasted_iota(jnp.int32, (1, 128), 1)
    result = jnp.zeros((1, 128), F32)
    for s in range(SURR):
        inside = (row_lane >= 16 * s) & (row_lane < 16 * s + 16)
        result = jnp.where(row_lane == s, jnp.max(jnp.where(inside, every, 0.0), axis=1, keepdims=True), result)
    out_peak[...] = result

    for h in range(2):
        target = h * 4 + lax.rem(z_low, 2) * 2 + lax.div(z_low, 2)

        @pl.when(target != k)
        def _():
            remote(block_rows.at[pl.ds(h * 16, 16)], chunks.at[k], chunk_send.at[h], chunk_recv, (col, target)).wait_send()

    @pl.when(hub)
    def _():
        await_sent(held.at[pl.ds(0, 8)], near_send)
        await_sent(held.at[pl.ds(0, 7)], relay_send)

    await_sent(angles.at[pl.ds(0, 7)], ang_send)
    await_sent(held.at[pl.ds(0, 12)], x_send)
    await_sent(kc.at[pl.ds(0, 3)], kc_send)
    await_sent(parts.at[pl.ds(0, 7)], part_send)
    await_sent(top1, t1_send)
    await_sent(top2, t2_send)


def body(series, slab_series, phase_index, basis):
    dma = pltpu.SemaphoreType.DMA
    vmem = pl.BlockSpec(memory_space=pltpu.VMEM)
    hbm = pl.BlockSpec(memory_space=pl.ANY)
    tile, peak = pl.pallas_call(
        kernel,
        out_shape=(pltpu.VMEM((64, 128), F32), pltpu.VMEM((1, 128), F32)),
        in_specs=[hbm, hbm, hbm, hbm],
        out_specs=(vmem, vmem),
        scratch_shapes=[
            pltpu.VMEM((TP, 768), BF16),
            pltpu.VMEM((4, FP, 128), F32),
            pltpu.VMEM((TP, TP), BF16),
            pltpu.VMEM((TP, TP), BF16),
            pltpu.VMEM((6, TP, 256), BF16),
            pltpu.VMEM((16, 16, TP), BF16),
            pltpu.VMEM((32, 150), F32),
            pltpu.VMEM((8, 16, 150), F32),
            pltpu.VMEM((8, SURR, 75), jnp.int32),
            pltpu.VMEM((256, TP), F32),
            pltpu.VMEM((1024, TP), BF16),
            pltpu.VMEM((1024, 128), F32),
            pltpu.VMEM((16, 128), F32),
            pltpu.VMEM((8, 16, 128), F32),
            pltpu.VMEM((1, 128), F32),
            pltpu.VMEM((31, 1, 128), F32),
            pltpu.VMEM((1, 128), F32),
            pltpu.VMEM((15, 1, 128), F32),
            dma((2,)), dma, dma, dma((2,)), dma, dma, dma, dma, dma, dma, dma((2,)), dma((4,)),
            dma, dma, dma, dma, dma, dma, dma, dma, pltpu.SemaphoreType.REGULAR,
        ],
        compiler_params=pltpu.CompilerParams(
            collective_id=0, has_side_effects=True, vmem_limit_bytes=56 * 1024 * 1024
        ),
        name="surrogate_peaks",
    )(series, slab_series.T, phase_index, basis)
    return tile.reshape(SURR, 2048)[:, :, None], peak[0, :SURR]


def solution(mesh):
    basis = basis_tables()

    def run(series, slab_series, phase_index):
        placed = (P(None, "col"), P("tm", "col"), P(None, "tm"), P())
        step = jax.shard_map(
            body, mesh=mesh, in_specs=placed, out_specs=(P(None, None, "col"), P()), check_vma=False
        )
        return step(series, slab_series, phase_index, jnp.asarray(basis))

    return run
```

```python
import functools
import math

import jax
import jax.numpy as jnp
import numpy as np
from jax import lax
from jax.experimental import pallas as pl
from jax.experimental.pallas import tpu as pltpu
from jax.sharding import PartitionSpec as P

FRAMES = 1200
FREQS = 600
FP = 640
TP = 1280
SURR = 4
COLS = 1536
EPS = 1e-6
F32 = jnp.float32
BF16 = jnp.bfloat16
MESH = pl.DeviceIdType.MESH
NEAR = (4, -4, 3, -3, 2, -2, 1, -1)
RING = (8, 7, -7, 6, -6, 5, -5, 4, -4, 3, -3, 2, -2, 1, -1)
PLANE = tuple((dx, dk) for dx in (2, 1, 3, 0) for dk in (4, 5, 3, 2, 6, 7, 1, 0) if (dx, dk) != (0, 0))


ORDER = np.concatenate([np.arange(2, 514, 2), np.arange(1, 513, 2), np.arange(514, 601, 2), np.arange(513, 600, 2)])
LAST = 555


def basis_tables():
    freq = np.concatenate([ORDER, np.ones(FP - FREQS, ORDER.dtype)])[:, None]
    lane = np.arange(128)[None, :]
    fine = 2.0 * np.pi * ((freq * lane) % FRAMES) / FRAMES
    step = np.broadcast_to(2.0 * np.pi * ((freq * 128) % FRAMES) / FRAMES, fine.shape)
    return np.stack([np.cos(fine), np.sin(fine), np.cos(step), np.sin(step)]).astype(np.float32)


def dot(a, b):
    return lax.dot_general(a, b, (((1,), (0,)), ((), ())), preferred_element_type=F32)


def dot_t(a, b):
    return lax.dot_general(a, b, (((1,), (1,)), ((), ())), preferred_element_type=F32)


def kernel(
    series, slab, phase, basis, out_tile, out_peak,
    cols, bas, thi, tlo, kc, held, block_rows, chunks, angles, spec, rot, best, mine, parts, own_top, top1, wide_top, top2,
    own_sem, col_sem, bas_sem, chunk_send, chunk_recv, ang_send, ang_recv, near_send, relay_send, x_send, x_recv, unit_recv,
    kc_send, kc_recv, part_send, part_recv, t1_send, t1_recv, t2_send, t2_recv, hello,
):
    col = lax.axis_index("col")
    k = lax.axis_index("tm")
    xx = lax.div(col, 16)
    z = lax.rem(col, 16)
    residue = lax.rem(k, 2) * 2 + lax.div(lax.rem(k, 4), 2)
    half = lax.div(k, 4)
    core = lax.rem(k, 2)
    z_low = lax.rem(z, 4)
    hub = z_low == residue

    def at_z(d):
        return (xx * 16 + lax.rem(z + d + 16, 16), k)

    def at_x(d):
        return (lax.rem(xx + d, 4) * 16 + z, k)

    def at_xk(dx, dk):
        return (lax.rem(xx + dx, 4) * 16 + z, lax.rem(k + dk, 8))

    def at_k(d):
        return (col, lax.rem(k + d, 8))

    def remote(src, dst, send, recv, dev):
        return pltpu.make_async_remote_copy(
            src_ref=src, dst_ref=dst, send_sem=send, recv_sem=recv, device_id=dev, device_id_type=MESH
        )

    def await_sent(ref, sem):
        remote(ref, ref, sem, sem, at_k(1)).wait_send()

    def await_all(ref, sem):
        remote(ref, ref, sem, sem, at_k(1)).wait_recv()

    def behind_of(d):
        return lax.div(lax.rem(z + d - residue + 32, 16), 4)

    behind = behind_of(0)

    def unit_to_z(rel, d):
        here = rel * 4 + xx
        there = lax.rem(behind + rel - behind_of(d) + 8, 4) * 4 + xx
        return here, there

    series_copy = pltpu.make_async_copy(
        series.at[:, pl.ds(pl.multiple_of(core * 768, 256), 768)], cols.at[pl.ds(0, FRAMES)], col_sem
    )
    basis_copy = pltpu.make_async_copy(basis, bas, bas_sem)
    own_phase = pltpu.make_async_copy(phase, angles.at[k], own_sem.at[0])
    own_chunk = pltpu.make_async_copy(slab, block_rows, own_sem.at[1])

    barrier = pltpu.get_barrier_semaphore()
    peers = [at_k(d) for d in range(1, 8)] + [at_x(d) for d in range(1, 4)] + [at_z(d) for d in (2, -2, 1, -1)]
    for dev in peers:
        pl.semaphore_signal(barrier, inc=1, device_id=dev, device_id_type=MESH)

    own_phase.start()
    own_chunk.start()
    basis_copy.start()
    series_copy.start()

    def make_rows(i, _):
        at = pl.multiple_of(i * 64, 64)
        sin_at = pl.multiple_of(FP + lax.rem(i + 2, 10) * 64, 64)
        c = bas[0, pl.ds(at, 64), :]
        s = bas[1, pl.ds(at, 64), :]
        sc = bas[2, pl.ds(at, 64), :]
        ss = bas[3, pl.ds(at, 64), :]
        for a in range(10):
            lanes = pl.ds(a * 128, 128)
            for rows, val in ((pl.ds(at, 64), c), (pl.ds(sin_at, 64), s)):
                hi = val.astype(BF16)
                thi[rows, lanes] = hi
                tlo[rows, lanes] = (val - hi.astype(F32)).astype(BF16)
            c, s = c * sc - s * ss, s * sc + c * ss
        return 0

    def norm_cols():
        def total(i, acc):
            x = cols[pl.ds(pl.multiple_of(i * 80, 16), 80), :].astype(F32)
            return acc + jnp.sum(x.reshape(10, 8, 768), axis=0)

        mean = jnp.sum(lax.fori_loop(0, 15, total, jnp.zeros((8, 768), F32)), axis=0, keepdims=True) * (1.0 / FRAMES)

        def squares(i, acc):
            x = cols[pl.ds(pl.multiple_of(i * 80, 16), 80), :].astype(F32) - mean
            return acc + jnp.sum((x * x).reshape(10, 8, 768), axis=0)

        scale = lax.rsqrt(jnp.sum(lax.fori_loop(0, 15, squares, jnp.zeros((8, 768), F32)), axis=0, keepdims=True) + EPS)

        def write(i, _):
            rows = pl.ds(pl.multiple_of(i * 80, 16), 80)
            cols[rows, :] = ((cols[rows, :].astype(F32) - mean) * scale).astype(BF16)
            return 0

        lax.fori_loop(0, 15, write, 0)

    def kc_copy(i):
        block = kc.at[core * 3 + i]
        return remote(block, block, kc_send, kc_recv, (col, k + 1 - 2 * core))

    def transform_cols(i):
        lanes = pl.ds(i * 256, 256)

        def block(b, _):
            rows = pl.ds(pl.multiple_of(b * 640, 128), 640)
            c = cols[:, lanes]
            kc[core * 3 + i, rows, :] = (dot(thi[rows, :], c) + dot(tlo[rows, :], c)).astype(BF16)
            return 0

        lax.fori_loop(0, 2, block, 0)
        kc_copy(i).start()

    own_chunk.wait()
    pl.semaphore_wait(barrier, 14)

    for h in range(2):
        target = h * 4 + lax.rem(z_low, 2) * 2 + lax.div(z_low, 2)

        @pl.when(target != k)
        def _():
            remote(block_rows.at[pl.ds(h * 16, 16)], chunks.at[k], chunk_send.at[h], chunk_recv, (col, target)).start()

    for d in (2, -2):
        pl.semaphore_signal(hello, inc=1, device_id=at_z(d), device_id_type=MESH)
    for d in range(1, 8):
        remote(phase, angles.at[k], ang_send, ang_recv, at_k(d)).start()

    basis_copy.wait()
    lax.fori_loop(0, 10, make_rows, 0)
    own_phase.wait()
    pl.semaphore_wait(hello, 2)

    def send_own(hops):
        for d in hops:
            here, there = unit_to_z(0, d)
            remote(held.at[here], held.at[there], near_send, unit_recv.at[lax.div(there, 4)], at_z(d)).start()

    @pl.when(hub)
    def _():
        chunks[k] = block_rows[pl.ds(pl.multiple_of(half * 16, 16), 16), :]
        await_all(chunks.at[pl.ds(0, 7)], chunk_recv)
        both = jnp.concatenate([chunks[i] + chunks[i + 4] for i in range(4)], axis=1)
        apart = jnp.concatenate([chunks[i] - chunks[i + 4] for i in range(4)], axis=1)
        both = both - jnp.sum(both, axis=1, keepdims=True) * (2.0 / FRAMES)
        rest = jnp.zeros((16, FP - FREQS), F32)
        held[xx] = jnp.concatenate([both, rest, apart, rest], axis=1).astype(BF16)
        send_own(NEAR)

    def arrived(rel):
        here = rel * 4 + xx
        remote(held.at[here], held.at[here], near_send, unit_recv.at[rel], at_z(1)).wait_recv()

    def relay_copies(rel):
        copies = []
        for d in (-3, -2, -1) if rel == 1 else (4, 3, 2, 1):
            here, there = unit_to_z(rel, d)
            copies.append(remote(held.at[here], held.at[there], relay_send, unit_recv.at[lax.div(there, 4)], at_z(d)))
        return copies

    def x_copies(rel, hops=(2, 1, 3)):
        here = rel * 4 + xx
        return [remote(held.at[here], held.at[here], x_send, x_recv.at[rel // 2], at_x(d)) for d in hops]

    def relay(rel):
        for copy in relay_copies(rel):
            copy.start()

    def forward(rel):
        for copy in x_copies(rel):
            copy.start()

    @pl.when(hub)
    def _():
        forward(0)

    cols[pl.ds(FRAMES, TP - FRAMES), :] = jnp.zeros((TP - FRAMES, 768), BF16)
    series_copy.wait()
    norm_cols()

    turned = lax.rem(lax.div(behind + 1, 2), 2)

    def neighbour(rel):
        arrived(rel)
        relay(rel)
        forward(rel)

    transform_cols(0)

    @pl.when(jnp.logical_not(hub))
    def _():
        arrived(0)
        forward(0)

    @pl.when(hub & (turned == 0))
    def _():
        neighbour(1)
        neighbour(3)

    @pl.when(hub & (turned == 1))
    def _():
        neighbour(3)
        neighbour(1)

    transform_cols(1)

    @pl.when(jnp.logical_not(hub))
    def _():
        arrived(1)
        forward(1)

    transform_cols(2)

    @pl.when(jnp.logical_not(hub))
    def _():
        arrived(3)
        x_copies(3, (2,))[0].start()
        arrived(2)
        x_copies(2, (2,))[0].start()
        for rel in (3, 2):
            for copy in x_copies(rel, (1, 3)):
                copy.start()

    @pl.when(hub)
    def _():
        arrived(2)
        forward(2)

    await_all(angles.at[pl.ds(0, 7)], ang_recv)
    turn = jnp.concatenate([angles[i] for i in range(8)] + [jnp.zeros((SURR, FP - FREQS), jnp.int32)], axis=1)
    digits = jnp.concatenate([lax.div(turn, 32), lax.rem(turn, 32)], axis=0).astype(F32).astype(BF16)
    source = lax.broadcasted_iota(jnp.int32, (FP, FP), 0) + 1
    place = lax.broadcasted_iota(jnp.int32, (FP, FP), 1)
    freq = 2 * place + jnp.where(
        place < 256, 2, jnp.where(place < 512, -511, jnp.where(place <= LAST, -510, jnp.where(place < FREQS, -599, FRAMES)))
    )
    moved = dot(digits, jnp.where(source == freq, 1.0, 0.0).astype(BF16))
    angle = (moved[:SURR] * 32.0 + moved[SURR:]) * (2.0 * math.pi / FRAMES)
    lane = lax.broadcasted_iota(jnp.int32, (SURR, FP), 1)
    weight = jnp.where(lane < FREQS, jnp.where(lane == LAST, 0.5, 1.0), 0.0).astype(F32)
    cos_phase = jnp.cos(angle) * weight
    sin_phase = jnp.sin(angle) * weight
    lane1 = lax.broadcasted_iota(jnp.int32, (1, FP), 1)
    inner = ((lane1 < FREQS) & (lane1 != LAST)).astype(F32)
    even_lane = lax.rem(lax.broadcasted_iota(jnp.int32, (128, 256), 1), 128) <= LAST - 512
    lane128 = lax.broadcasted_iota(jnp.int32, (256, 128), 1)
    row16 = lax.rem(lax.broadcasted_iota(jnp.int32, (256, 128), 0), 16)

    def spectra(h):
        await_all(held.at[pl.ds(0, 6)], x_recv.at[h])
        rows = pl.ds(128 * h, 128)
        both = held[8 * h : 8 * h + 8, :, 0:FP].reshape(128, FP)
        apart = held[8 * h : 8 * h + 8, :, FP:TP].reshape(128, FP)

        def spectrum(x, start):
            table = pl.ds(start, 256)
            return dot_t(x, thi[table, 0:FP]) + dot_t(x, tlo[table, 0:FP])

        for start in (0, 768):
            spec[rows, start : start + 256] = spectrum(both, start)
            spec[rows, start + 256 : start + 512] = spectrum(apart, start + 256)
        spec[rows, 512:768] = jnp.where(even_lane, spectrum(both, 512), spectrum(apart, 512))

    def halves(rows):
        sc = spec[rows, 0:FP]
        ss = jnp.concatenate([spec[rows, 768:TP], spec[rows, FP:768]], axis=1)
        return sc, ss

    def rotate(h, s):
        sc, ss = halves(pl.ds(128 * h, 128))
        cp = cos_phase[s : s + 1, :]
        sp = sin_phase[s : s + 1, :]
        rows = pl.ds(s * 256 + 128 * h, 128)
        rot[rows, 0:FP] = (sc * cp + ss * sp).astype(BF16)
        turned_back = (ss * cp - sc * sp).astype(BF16)
        rot[rows, 768:TP] = turned_back[:, 0:512]
        rot[rows, FP:768] = turned_back[:, 512:FP]

    spectra(0)
    for s in range(SURR):
        rotate(0, s)
    await_all(kc.at[pl.ds(0, 3)], kc_recv)
    spectra(1)
    sc, ss = halves(pl.ds(0, 256))
    power = jnp.sum((sc * sc + ss * ss) * inner, axis=1, keepdims=True)
    last = jnp.sum(jnp.where(lane1 == LAST, sc, 0.0), axis=1, keepdims=True)
    scales = []
    for s in range(SURR):
        end = 2.0 * cos_phase[s : s + 1, LAST : LAST + 1] * last
        energy = power * (2.0 / FRAMES) + end * end * (1.0 / FRAMES)
        scales.append(lax.rsqrt(energy + EPS) * (math.sqrt(FRAMES) * 2.0 / FRAMES))
    for s in range(SURR):
        rotate(1, s)
        rows = pl.ds(s * 256, 256)
        for j in range(6):
            score = jnp.abs(dot(rot[rows, :], kc[j]))
            score = jnp.maximum(score[:, :128], score[:, 128:])
            best[rows, :] = score if j == 0 else jnp.maximum(best[rows, :], score)
    placed = jnp.zeros((256, 128), F32)
    for s in range(SURR):
        top = jnp.max(best[pl.ds(s * 256, 256), :], axis=1, keepdims=True) * scales[s]
        placed = jnp.where(lane128 == row16 + 16 * s, top, placed)
    found = jnp.max(placed.reshape(16, 16, 128), axis=1)
    for n in range(16):
        row = (n % 4) * 4 + lax.rem(behind + n // 4, 4)
        mine[pl.ds(row, 1), :] = found[n : n + 1, :]

    own_top[...] = jnp.max(mine[...], axis=0, keepdims=True)
    for n, (dx, dk) in enumerate(PLANE):
        remote(own_top, top1.at[n], t1_send, t1_recv, at_xk(dx, dk)).start()
    for d in range(1, 8):
        remote(mine, parts.at[k], part_send, part_recv, at_k(d)).start()
    parts[k] = mine[...]
    await_all(top1, t1_recv)
    wide_top[...] = jnp.maximum(own_top[...], jnp.max(top1[...], axis=0))
    for n, d in enumerate(RING):
        remote(wide_top, top2.at[n], t2_send, t2_recv, at_z(d)).start()
    await_all(parts.at[pl.ds(0, 7)], part_recv)
    lane16 = lax.broadcasted_iota(jnp.int32, (16, 128), 1)
    for s in range(SURR):
        full = jnp.zeros((16, 128), F32)
        for kk in range(8):
            place = (kk % 2 * 2 + kk % 4 // 2) * 32 + (kk // 4) * 16
            moved = pltpu.roll(parts[kk], (place - 16 * s) % 128, 1)
            full = jnp.where((lane16 >= place) & (lane16 < place + 16), moved, full)
        out_tile[pl.ds(s * 16, 16), :] = full
    await_all(top2, t2_recv)
    every = jnp.maximum(wide_top[...], jnp.max(top2[...], axis=0))
    row_lane = lax.broadcasted_iota(jnp.int32, (1, 128), 1)
    result = jnp.zeros((1, 128), F32)
    for s in range(SURR):
        inside = (row_lane >= 16 * s) & (row_lane < 16 * s + 16)
        result = jnp.where(row_lane == s, jnp.max(jnp.where(inside, every, 0.0), axis=1, keepdims=True), result)
    out_peak[...] = result

    for h in range(2):
        target = h * 4 + lax.rem(z_low, 2) * 2 + lax.div(z_low, 2)

        @pl.when(target != k)
        def _():
            remote(block_rows.at[pl.ds(h * 16, 16)], chunks.at[k], chunk_send.at[h], chunk_recv, (col, target)).wait_send()

    @pl.when(hub)
    def _():
        await_sent(held.at[pl.ds(0, 8)], near_send)
        await_sent(held.at[pl.ds(0, 7)], relay_send)

    await_sent(angles.at[pl.ds(0, 7)], ang_send)
    await_sent(held.at[pl.ds(0, 12)], x_send)
    await_sent(kc.at[pl.ds(0, 3)], kc_send)
    await_sent(parts.at[pl.ds(0, 7)], part_send)
    await_sent(top1, t1_send)
    await_sent(top2, t2_send)


def body(series, slab_series, phase_index, basis):
    dma = pltpu.SemaphoreType.DMA
    vmem = pl.BlockSpec(memory_space=pltpu.VMEM)
    hbm = pl.BlockSpec(memory_space=pl.ANY)
    tile, peak = pl.pallas_call(
        kernel,
        out_shape=(pltpu.VMEM((64, 128), F32), pltpu.VMEM((1, 128), F32)),
        in_specs=[hbm, hbm, hbm, hbm],
        out_specs=(vmem, vmem),
        scratch_shapes=[
            pltpu.VMEM((TP, 768), BF16),
            pltpu.VMEM((4, FP, 128), F32),
            pltpu.VMEM((TP, TP), BF16),
            pltpu.VMEM((TP, TP), BF16),
            pltpu.VMEM((6, TP, 256), BF16),
            pltpu.VMEM((16, 16, TP), BF16),
            pltpu.VMEM((32, 150), F32),
            pltpu.VMEM((8, 16, 150), F32),
            pltpu.VMEM((8, SURR, 75), jnp.int32),
            pltpu.VMEM((256, TP), F32),
            pltpu.VMEM((1024, TP), BF16),
            pltpu.VMEM((1024, 128), F32),
            pltpu.VMEM((16, 128), F32),
            pltpu.VMEM((8, 16, 128), F32),
            pltpu.VMEM((1, 128), F32),
            pltpu.VMEM((31, 1, 128), F32),
            pltpu.VMEM((1, 128), F32),
            pltpu.VMEM((15, 1, 128), F32),
            dma((2,)), dma, dma, dma((2,)), dma, dma, dma, dma, dma, dma, dma((2,)), dma((4,)),
            dma, dma, dma, dma, dma, dma, dma, dma, pltpu.SemaphoreType.REGULAR,
        ],
        compiler_params=pltpu.CompilerParams(
            collective_id=0, has_side_effects=True, vmem_limit_bytes=56 * 1024 * 1024
        ),
        name="surrogate_peaks",
    )(series, slab_series.T, phase_index, basis)
    return tile.reshape(SURR, 2048)[:, :, None], peak[0, :SURR]


def solution(mesh):
    basis = basis_tables()

    def run(series, slab_series, phase_index):
        placed = (P(None, "col"), P("tm", "col"), P(None, "tm"), P())
        step = jax.shard_map(
            body, mesh=mesh, in_specs=placed, out_specs=(P(None, None, "col"), P()), check_vma=False
        )
        return step(series, slab_series, phase_index, jnp.asarray(basis))

    return run
```

```python
import functools
import math

import jax
import jax.numpy as jnp
import numpy as np
from jax import lax
from jax.experimental import pallas as pl
from jax.experimental.pallas import tpu as pltpu
from jax.sharding import PartitionSpec as P

FRAMES = 1200
FREQS = 600
FP = 640
TP = 1280
SURR = 4
COLS = 1536
EPS = 1e-6
F32 = jnp.float32
BF16 = jnp.bfloat16
MESH = pl.DeviceIdType.MESH
NEAR = (4, -4, 3, -3, 2, -2, 1, -1)
RING = (8, 7, -7, 6, -6, 5, -5, 4, -4, 3, -3, 2, -2, 1, -1)
PLANE = tuple((dx, dk) for dx in (2, 1, 3, 0) for dk in (4, 5, 3, 2, 6, 7, 1, 0) if (dx, dk) != (0, 0))


ORDER = np.concatenate([np.arange(2, 514, 2), np.arange(1, 513, 2), np.arange(514, 601, 2), np.arange(513, 600, 2)])
LAST = 555


def basis_tables():
    freq = np.concatenate([ORDER, np.ones(FP - FREQS, ORDER.dtype)])[:, None]
    lane = np.arange(128)[None, :]
    fine = 2.0 * np.pi * ((freq * lane) % FRAMES) / FRAMES
    step = np.broadcast_to(2.0 * np.pi * ((freq * 128) % FRAMES) / FRAMES, fine.shape)
    return np.stack([np.cos(fine), np.sin(fine), np.cos(step), np.sin(step)]).astype(np.float32)


def dot(a, b):
    return lax.dot_general(a, b, (((1,), (0,)), ((), ())), preferred_element_type=F32)


def dot_t(a, b):
    return lax.dot_general(a, b, (((1,), (1,)), ((), ())), preferred_element_type=F32)


def kernel(
    series, slab, phase, basis, out_tile, out_peak,
    cols, bas, thi, tlo, kc, held, block_rows, chunks, angles, spec, rot, mine, parts, own_top, top1, wide_top, top2,
    own_sem, col_sem, bas_sem, chunk_send, chunk_recv, ang_send, ang_recv, near_send, relay_send, x_send, x_recv, unit_recv,
    kc_send, kc_recv, part_send, part_recv, t1_send, t1_recv, t2_send, t2_recv, hello,
):
    col = lax.axis_index("col")
    k = lax.axis_index("tm")
    xx = lax.div(col, 16)
    z = lax.rem(col, 16)
    residue = lax.rem(k, 2) * 2 + lax.div(lax.rem(k, 4), 2)
    half = lax.div(k, 4)
    core = lax.rem(k, 2)
    z_low = lax.rem(z, 4)
    hub = z_low == residue

    def at_z(d):
        return (xx * 16 + lax.rem(z + d + 16, 16), k)

    def at_x(d):
        return (lax.rem(xx + d, 4) * 16 + z, k)

    def at_xk(dx, dk):
        return (lax.rem(xx + dx, 4) * 16 + z, lax.rem(k + dk, 8))

    def at_k(d):
        return (col, lax.rem(k + d, 8))

    def remote(src, dst, send, recv, dev):
        return pltpu.make_async_remote_copy(
            src_ref=src, dst_ref=dst, send_sem=send, recv_sem=recv, device_id=dev, device_id_type=MESH
        )

    def await_sent(ref, sem):
        remote(ref, ref, sem, sem, at_k(1)).wait_send()

    def await_all(ref, sem):
        remote(ref, ref, sem, sem, at_k(1)).wait_recv()

    def behind_of(d):
        return lax.div(lax.rem(z + d - residue + 32, 16), 4)

    behind = behind_of(0)

    def unit_to_z(rel, d):
        here = rel * 4 + xx
        there = lax.rem(behind + rel - behind_of(d) + 8, 4) * 4 + xx
        return here, there

    series_copy = pltpu.make_async_copy(
        series.at[:, pl.ds(pl.multiple_of(core * 768, 256), 768)], cols.at[pl.ds(0, FRAMES)], col_sem
    )
    basis_copy = pltpu.make_async_copy(basis, bas, bas_sem)
    own_phase = pltpu.make_async_copy(phase, angles.at[k], own_sem.at[0])
    own_chunk = pltpu.make_async_copy(slab, block_rows, own_sem.at[1])

    barrier = pltpu.get_barrier_semaphore()
    peers = [at_k(d) for d in range(1, 8)] + [at_x(d) for d in range(1, 4)] + [at_z(d) for d in (2, -2, 1, -1)]
    for dev in peers:
        pl.semaphore_signal(barrier, inc=1, device_id=dev, device_id_type=MESH)

    own_phase.start()
    own_chunk.start()
    basis_copy.start()
    series_copy.start()

    def make_rows(i, _):
        at = pl.multiple_of(i * 64, 64)
        sin_at = pl.multiple_of(FP + lax.rem(i + 2, 10) * 64, 64)
        c = bas[0, pl.ds(at, 64), :]
        s = bas[1, pl.ds(at, 64), :]
        sc = bas[2, pl.ds(at, 64), :]
        ss = bas[3, pl.ds(at, 64), :]
        for a in range(10):
            lanes = pl.ds(a * 128, 128)
            for rows, val in ((pl.ds(at, 64), c), (pl.ds(sin_at, 64), s)):
                hi = val.astype(BF16)
                thi[rows, lanes] = hi
                tlo[rows, lanes] = (val - hi.astype(F32)).astype(BF16)
            c, s = c * sc - s * ss, s * sc + c * ss
        return 0

    def norm_cols():
        def total(i, acc):
            x = cols[pl.ds(pl.multiple_of(i * 80, 16), 80), :].astype(F32)
            return acc + jnp.sum(x.reshape(10, 8, 768), axis=0)

        mean = jnp.sum(lax.fori_loop(0, 15, total, jnp.zeros((8, 768), F32)), axis=0, keepdims=True) * (1.0 / FRAMES)

        def squares(i, acc):
            x = cols[pl.ds(pl.multiple_of(i * 80, 16), 80), :].astype(F32) - mean
            return acc + jnp.sum((x * x).reshape(10, 8, 768), axis=0)

        scale = lax.rsqrt(jnp.sum(lax.fori_loop(0, 15, squares, jnp.zeros((8, 768), F32)), axis=0, keepdims=True) + EPS)

        def write(i, _):
            rows = pl.ds(pl.multiple_of(i * 80, 16), 80)
            cols[rows, :] = ((cols[rows, :].astype(F32) - mean) * scale).astype(BF16)
            return 0

        lax.fori_loop(0, 15, write, 0)

    def kc_copy(i):
        block = kc.at[core * 3 + i]
        return remote(block, block, kc_send, kc_recv, (col, k + 1 - 2 * core))

    def transform_cols(i):
        lanes = pl.ds(i * 256, 256)

        def block(b, _):
            rows = pl.ds(pl.multiple_of(b * 640, 128), 640)
            c = cols[:, lanes]
            kc[core * 3 + i, rows, :] = (dot(thi[rows, :], c) + dot(tlo[rows, :], c)).astype(BF16)
            return 0

        lax.fori_loop(0, 2, block, 0)
        kc_copy(i).start()

    own_chunk.wait()
    pl.semaphore_wait(barrier, 14)

    for h in range(2):
        target = h * 4 + lax.rem(z_low, 2) * 2 + lax.div(z_low, 2)

        @pl.when(target != k)
        def _():
            remote(block_rows.at[pl.ds(h * 16, 16)], chunks.at[k], chunk_send.at[h], chunk_recv, (col, target)).start()

    for d in (2, -2):
        pl.semaphore_signal(hello, inc=1, device_id=at_z(d), device_id_type=MESH)
    for d in range(1, 8):
        remote(phase, angles.at[k], ang_send, ang_recv, at_k(d)).start()

    basis_copy.wait()
    lax.fori_loop(0, 10, make_rows, 0)
    own_phase.wait()
    pl.semaphore_wait(hello, 2)

    def send_own(hops):
        for d in hops:
            here, there = unit_to_z(0, d)
            remote(held.at[here], held.at[there], near_send, unit_recv.at[lax.div(there, 4)], at_z(d)).start()

    @pl.when(hub)
    def _():
        chunks[k] = block_rows[pl.ds(pl.multiple_of(half * 16, 16), 16), :]
        await_all(chunks.at[pl.ds(0, 7)], chunk_recv)
        both = jnp.concatenate([chunks[i] + chunks[i + 4] for i in range(4)], axis=1)
        apart = jnp.concatenate([chunks[i] - chunks[i + 4] for i in range(4)], axis=1)
        both = both - jnp.sum(both, axis=1, keepdims=True) * (2.0 / FRAMES)
        rest = jnp.zeros((16, FP - FREQS), F32)
        held[xx] = jnp.concatenate([both, rest, apart, rest], axis=1).astype(BF16)
        send_own(NEAR)

    def arrived(rel):
        here = rel * 4 + xx
        remote(held.at[here], held.at[here], near_send, unit_recv.at[rel], at_z(1)).wait_recv()

    def relay_copies(rel):
        copies = []
        for d in (-3, -2, -1) if rel == 1 else (4, 3, 2, 1):
            here, there = unit_to_z(rel, d)
            copies.append(remote(held.at[here], held.at[there], relay_send, unit_recv.at[lax.div(there, 4)], at_z(d)))
        return copies

    def x_copies(rel, hops=(2, 1, 3)):
        here = rel * 4 + xx
        return [remote(held.at[here], held.at[here], x_send, x_recv.at[rel // 2], at_x(d)) for d in hops]

    def relay(rel):
        for copy in relay_copies(rel):
            copy.start()

    def forward(rel):
        for copy in x_copies(rel):
            copy.start()

    @pl.when(hub)
    def _():
        forward(0)

    cols[pl.ds(FRAMES, TP - FRAMES), :] = jnp.zeros((TP - FRAMES, 768), BF16)
    series_copy.wait()
    norm_cols()

    turned = lax.rem(lax.div(behind + 1, 2), 2)

    def neighbour(rel):
        arrived(rel)
        relay(rel)
        forward(rel)

    transform_cols(0)

    @pl.when(jnp.logical_not(hub))
    def _():
        arrived(0)
        forward(0)

    @pl.when(hub & (turned == 0))
    def _():
        neighbour(1)
        neighbour(3)

    @pl.when(hub & (turned == 1))
    def _():
        neighbour(3)
        neighbour(1)

    transform_cols(1)

    @pl.when(jnp.logical_not(hub))
    def _():
        arrived(1)
        forward(1)

    transform_cols(2)

    @pl.when(jnp.logical_not(hub))
    def _():
        arrived(3)
        x_copies(3, (2,))[0].start()
        arrived(2)
        x_copies(2, (2,))[0].start()
        for rel in (3, 2):
            for copy in x_copies(rel, (1, 3)):
                copy.start()

    @pl.when(hub)
    def _():
        arrived(2)
        forward(2)

    await_all(angles.at[pl.ds(0, 7)], ang_recv)
    turn = jnp.concatenate([angles[i] for i in range(8)] + [jnp.zeros((SURR, FP - FREQS), jnp.int32)], axis=1)
    digits = jnp.concatenate([lax.div(turn, 32), lax.rem(turn, 32)], axis=0).astype(F32).astype(BF16)
    source = lax.broadcasted_iota(jnp.int32, (FP, FP), 0) + 1
    place = lax.broadcasted_iota(jnp.int32, (FP, FP), 1)
    freq = 2 * place + jnp.where(
        place < 256, 2, jnp.where(place < 512, -511, jnp.where(place <= LAST, -510, jnp.where(place < FREQS, -599, FRAMES)))
    )
    moved = dot(digits, jnp.where(source == freq, 1.0, 0.0).astype(BF16))
    angle = (moved[:SURR] * 32.0 + moved[SURR:]) * (2.0 * math.pi / FRAMES)
    lane = lax.broadcasted_iota(jnp.int32, (SURR, FP), 1)
    weight = jnp.where(lane < FREQS, jnp.where(lane == LAST, 0.5, 1.0), 0.0).astype(F32)
    cos_phase = jnp.cos(angle) * weight
    sin_phase = jnp.sin(angle) * weight
    lane1 = lax.broadcasted_iota(jnp.int32, (1, FP), 1)
    inner = ((lane1 < FREQS) & (lane1 != LAST)).astype(F32)
    even_lane = lax.rem(lax.broadcasted_iota(jnp.int32, (128, 256), 1), 128) <= LAST - 512
    lane128 = lax.broadcasted_iota(jnp.int32, (256, 128), 1)
    row16 = lax.rem(lax.broadcasted_iota(jnp.int32, (256, 128), 0), 16)

    def spectra(h):
        await_all(held.at[pl.ds(0, 6)], x_recv.at[h])
        rows = pl.ds(128 * h, 128)
        both = held[8 * h : 8 * h + 8, :, 0:FP].reshape(128, FP)
        apart = held[8 * h : 8 * h + 8, :, FP:TP].reshape(128, FP)

        def spectrum(x, start):
            table = pl.ds(start, 256)
            return dot_t(x, thi[table, 0:FP]) + dot_t(x, tlo[table, 0:FP])

        for start in (0, 768):
            spec[rows, start : start + 256] = spectrum(both, start)
            spec[rows, start + 256 : start + 512] = spectrum(apart, start + 256)
        spec[rows, 512:768] = jnp.where(even_lane, spectrum(both, 512), spectrum(apart, 512))

    def halves(rows):
        sc = spec[rows, 0:FP]
        ss = jnp.concatenate([spec[rows, 768:TP], spec[rows, FP:768]], axis=1)
        return sc, ss

    def power(h):
        sc, ss = halves(pl.ds(128 * h, 128))
        inside = jnp.sum((sc * sc + ss * ss) * inner, axis=1, keepdims=True)
        return inside, jnp.sum(jnp.where(lane1 == LAST, sc, 0.0), axis=1, keepdims=True)

    def rotate(h, s):
        sc, ss = halves(pl.ds(128 * h, 128))
        cp = cos_phase[s : s + 1, :]
        sp = sin_phase[s : s + 1, :]
        rows = pl.ds(s * 256 + 128 * h, 128)
        rot[rows, 0:FP] = (sc * cp + ss * sp).astype(BF16)
        turned_back = (ss * cp - sc * sp).astype(BF16)
        rot[rows, 768:TP] = turned_back[:, 0:512]
        rot[rows, FP:768] = turned_back[:, 512:FP]

    spectra(0)
    powers = [power(0)]
    for s in range(SURR):
        rotate(0, s)
    await_all(kc.at[pl.ds(0, 3)], kc_recv)
    spectra(1)
    powers.append(power(1))
    scales = []
    for s in range(SURR):
        energy = []
        for inside, last in powers:
            end = 2.0 * cos_phase[s : s + 1, LAST : LAST + 1] * last
            energy.append(inside * (2.0 / FRAMES) + end * end * (1.0 / FRAMES))
        scales.append(lax.rsqrt(jnp.concatenate(energy, axis=0) + EPS) * (math.sqrt(FRAMES) * 2.0 / FRAMES))
    placed = jnp.zeros((256, 128), F32)
    for s in range(SURR):
        rotate(1, s)
        rows = pl.ds(s * 256, 256)
        for j in range(6):
            score = jnp.abs(dot(rot[rows, :], kc[j]))
            score = jnp.maximum(score[:, :128], score[:, 128:])
            tops = score if j == 0 else jnp.maximum(tops, score)
        placed = jnp.where(lane128 == row16 + 16 * s, jnp.max(tops, axis=1, keepdims=True) * scales[s], placed)
    found = jnp.max(placed.reshape(16, 16, 128), axis=1)
    for n in range(16):
        row = (n % 4) * 4 + lax.rem(behind + n // 4, 4)
        mine[pl.ds(row, 1), :] = found[n : n + 1, :]

    own_top[...] = jnp.max(mine[...], axis=0, keepdims=True)
    for n, (dx, dk) in enumerate(PLANE):
        remote(own_top, top1.at[n], t1_send, t1_recv, at_xk(dx, dk)).start()
    for d in range(1, 8):
        remote(mine, parts.at[k], part_send, part_recv, at_k(d)).start()
    parts[k] = mine[...]
    await_all(top1, t1_recv)
    wide_top[...] = jnp.maximum(own_top[...], jnp.max(top1[...], axis=0))
    for n, d in enumerate(RING):
        remote(wide_top, top2.at[n], t2_send, t2_recv, at_z(d)).start()
    await_all(parts.at[pl.ds(0, 7)], part_recv)
    lane16 = lax.broadcasted_iota(jnp.int32, (16, 128), 1)
    for s in range(SURR):
        full = jnp.zeros((16, 128), F32)
        for kk in range(8):
            place = (kk % 2 * 2 + kk % 4 // 2) * 32 + (kk // 4) * 16
            moved = pltpu.roll(parts[kk], (place - 16 * s) % 128, 1)
            full = jnp.where((lane16 >= place) & (lane16 < place + 16), moved, full)
        out_tile[pl.ds(s * 16, 16), :] = full
    await_all(top2, t2_recv)
    every = jnp.maximum(wide_top[...], jnp.max(top2[...], axis=0))
    row_lane = lax.broadcasted_iota(jnp.int32, (1, 128), 1)
    result = jnp.zeros((1, 128), F32)
    for s in range(SURR):
        inside = (row_lane >= 16 * s) & (row_lane < 16 * s + 16)
        result = jnp.where(row_lane == s, jnp.max(jnp.where(inside, every, 0.0), axis=1, keepdims=True), result)
    out_peak[...] = result

    for h in range(2):
        target = h * 4 + lax.rem(z_low, 2) * 2 + lax.div(z_low, 2)

        @pl.when(target != k)
        def _():
            remote(block_rows.at[pl.ds(h * 16, 16)], chunks.at[k], chunk_send.at[h], chunk_recv, (col, target)).wait_send()

    @pl.when(hub)
    def _():
        await_sent(held.at[pl.ds(0, 8)], near_send)
        await_sent(held.at[pl.ds(0, 7)], relay_send)

    await_sent(angles.at[pl.ds(0, 7)], ang_send)
    await_sent(held.at[pl.ds(0, 12)], x_send)
    await_sent(kc.at[pl.ds(0, 3)], kc_send)
    await_sent(parts.at[pl.ds(0, 7)], part_send)
    await_sent(top1, t1_send)
    await_sent(top2, t2_send)


def body(series, slab_series, phase_index, basis):
    dma = pltpu.SemaphoreType.DMA
    vmem = pl.BlockSpec(memory_space=pltpu.VMEM)
    hbm = pl.BlockSpec(memory_space=pl.ANY)
    tile, peak = pl.pallas_call(
        kernel,
        out_shape=(pltpu.VMEM((64, 128), F32), pltpu.VMEM((1, 128), F32)),
        in_specs=[hbm, hbm, hbm, hbm],
        out_specs=(vmem, vmem),
        scratch_shapes=[
            pltpu.VMEM((TP, 768), BF16),
            pltpu.VMEM((4, FP, 128), F32),
            pltpu.VMEM((TP, TP), BF16),
            pltpu.VMEM((TP, TP), BF16),
            pltpu.VMEM((6, TP, 256), BF16),
            pltpu.VMEM((16, 16, TP), BF16),
            pltpu.VMEM((32, 150), F32),
            pltpu.VMEM((8, 16, 150), F32),
            pltpu.VMEM((8, SURR, 75), jnp.int32),
            pltpu.VMEM((256, TP), F32),
            pltpu.VMEM((1024, TP), BF16),
            pltpu.VMEM((16, 128), F32),
            pltpu.VMEM((8, 16, 128), F32),
            pltpu.VMEM((1, 128), F32),
            pltpu.VMEM((31, 1, 128), F32),
            pltpu.VMEM((1, 128), F32),
            pltpu.VMEM((15, 1, 128), F32),
            dma((2,)), dma, dma, dma((2,)), dma, dma, dma, dma, dma, dma, dma((2,)), dma((4,)),
            dma, dma, dma, dma, dma, dma, dma, dma, pltpu.SemaphoreType.REGULAR,
        ],
        compiler_params=pltpu.CompilerParams(
            collective_id=0, has_side_effects=True, vmem_limit_bytes=56 * 1024 * 1024
        ),
        name="surrogate_peaks",
    )(series, slab_series.T, phase_index, basis)
    return tile.reshape(SURR, 2048)[:, :, None], peak[0, :SURR]


def solution(mesh):
    basis = basis_tables()

    def run(series, slab_series, phase_index):
        placed = (P(None, "col"), P("tm", "col"), P(None, "tm"), P())
        step = jax.shard_map(
            body, mesh=mesh, in_specs=placed, out_specs=(P(None, None, "col"), P()), check_vma=False
        )
        return step(series, slab_series, phase_index, jnp.asarray(basis))

    return run
```

```python
import functools
import math

import jax
import jax.numpy as jnp
import numpy as np
from jax import lax
from jax.experimental import pallas as pl
from jax.experimental.pallas import tpu as pltpu
from jax.sharding import PartitionSpec as P

FRAMES = 1200
FREQS = 600
FP = 640
TP = 1280
SURR = 4
COLS = 1536
EPS = 1e-6
F32 = jnp.float32
BF16 = jnp.bfloat16
MESH = pl.DeviceIdType.MESH
NEAR = (4, -4, 3, -3, 2, -2, 1, -1)
RING = (8, 7, -7, 6, -6, 5, -5, 4, -4, 3, -3, 2, -2, 1, -1)
PLANE = tuple((dx, dk) for dx in (2, 1, 3, 0) for dk in (4, 5, 3, 2, 6, 7, 1, 0) if (dx, dk) != (0, 0))


ORDER = np.concatenate([np.arange(2, 514, 2), np.arange(1, 513, 2), np.arange(514, 601, 2), np.arange(513, 600, 2)])
LAST = 555


def basis_tables():
    freq = np.concatenate([ORDER, np.ones(FP - FREQS, ORDER.dtype)])[:, None]
    lane = np.arange(128)[None, :]
    fine = 2.0 * np.pi * ((freq * lane) % FRAMES) / FRAMES
    step = np.broadcast_to(2.0 * np.pi * ((freq * 128) % FRAMES) / FRAMES, fine.shape)
    return np.stack([np.cos(fine), np.sin(fine), np.cos(step), np.sin(step)]).astype(np.float32)


def dot(a, b):
    return lax.dot_general(a, b, (((1,), (0,)), ((), ())), preferred_element_type=F32)


def dot_t(a, b):
    return lax.dot_general(a, b, (((1,), (1,)), ((), ())), preferred_element_type=F32)


def kernel(
    series, slab, phase, basis, out_tile, out_peak,
    cols, bas, thi, tlo, kc, held, block_rows, chunks, angles, spec, rot, mine, parts, own_top, top1, wide_top, top2,
    own_sem, col_sem, bas_sem, chunk_send, chunk_recv, ang_send, ang_recv, near_send, relay_send, x_send, x_recv, unit_recv,
    kc_send, kc_recv, part_send, part_recv, t1_send, t1_recv, t2_send, t2_recv, hello,
):
    col = lax.axis_index("col")
    k = lax.axis_index("tm")
    xx = lax.div(col, 16)
    z = lax.rem(col, 16)
    residue = lax.rem(k, 2) * 2 + lax.div(lax.rem(k, 4), 2)
    half = lax.div(k, 4)
    core = lax.rem(k, 2)
    z_low = lax.rem(z, 4)
    hub = z_low == residue

    def at_z(d):
        return (xx * 16 + lax.rem(z + d + 16, 16), k)

    def at_x(d):
        return (lax.rem(xx + d, 4) * 16 + z, k)

    def at_xk(dx, dk):
        return (lax.rem(xx + dx, 4) * 16 + z, lax.rem(k + dk, 8))

    def at_k(d):
        return (col, lax.rem(k + d, 8))

    def remote(src, dst, send, recv, dev):
        return pltpu.make_async_remote_copy(
            src_ref=src, dst_ref=dst, send_sem=send, recv_sem=recv, device_id=dev, device_id_type=MESH
        )

    def await_sent(ref, sem):
        remote(ref, ref, sem, sem, at_k(1)).wait_send()

    def await_all(ref, sem):
        remote(ref, ref, sem, sem, at_k(1)).wait_recv()

    def behind_of(d):
        return lax.div(lax.rem(z + d - residue + 32, 16), 4)

    behind = behind_of(0)

    def unit_to_z(rel, d):
        here = rel * 4 + xx
        there = lax.rem(behind + rel - behind_of(d) + 8, 4) * 4 + xx
        return here, there

    series_copy = pltpu.make_async_copy(
        series.at[:, pl.ds(pl.multiple_of(core * 768, 256), 768)], cols.at[pl.ds(0, FRAMES)], col_sem
    )
    basis_copy = pltpu.make_async_copy(basis, bas, bas_sem)
    own_phase = pltpu.make_async_copy(phase, angles.at[k], own_sem.at[0])
    own_chunk = pltpu.make_async_copy(slab, block_rows, own_sem.at[1])

    barrier = pltpu.get_barrier_semaphore()
    peers = [at_k(d) for d in range(1, 8)] + [at_x(d) for d in range(1, 4)] + [at_z(d) for d in (2, -2, 1, -1)]
    for dev in peers:
        pl.semaphore_signal(barrier, inc=1, device_id=dev, device_id_type=MESH)

    own_phase.start()
    own_chunk.start()
    basis_copy.start()
    series_copy.start()

    def make_rows(i, _):
        at = pl.multiple_of(i * 64, 64)
        sin_at = pl.multiple_of(FP + lax.rem(i + 2, 10) * 64, 64)
        c = bas[0, pl.ds(at, 64), :]
        s = bas[1, pl.ds(at, 64), :]
        sc = bas[2, pl.ds(at, 64), :]
        ss = bas[3, pl.ds(at, 64), :]
        for a in range(10):
            lanes = pl.ds(a * 128, 128)
            for rows, val in ((pl.ds(at, 64), c), (pl.ds(sin_at, 64), s)):
                hi = val.astype(BF16)
                thi[rows, lanes] = hi
                tlo[rows, lanes] = (val - hi.astype(F32)).astype(BF16)
            c, s = c * sc - s * ss, s * sc + c * ss
        return 0

    def norm_cols():
        def total(i, acc):
            x = cols[pl.ds(pl.multiple_of(i * 80, 16), 80), :].astype(F32)
            return acc + jnp.sum(x.reshape(10, 8, 768), axis=0)

        mean = jnp.sum(lax.fori_loop(0, 15, total, jnp.zeros((8, 768), F32)), axis=0, keepdims=True) * (1.0 / FRAMES)

        def squares(i, acc):
            x = cols[pl.ds(pl.multiple_of(i * 80, 16), 80), :].astype(F32) - mean
            return acc + jnp.sum((x * x).reshape(10, 8, 768), axis=0)

        scale = lax.rsqrt(jnp.sum(lax.fori_loop(0, 15, squares, jnp.zeros((8, 768), F32)), axis=0, keepdims=True) + EPS)

        def write(i, _):
            rows = pl.ds(pl.multiple_of(i * 80, 16), 80)
            cols[rows, :] = ((cols[rows, :].astype(F32) - mean) * scale).astype(BF16)
            return 0

        lax.fori_loop(0, 15, write, 0)

    def kc_copy(i):
        block = kc.at[core * 3 + i]
        return remote(block, block, kc_send, kc_recv, (col, k + 1 - 2 * core))

    def transform_cols(i):
        lanes = pl.ds(i * 256, 256)

        def block(b, _):
            rows = pl.ds(pl.multiple_of(b * 640, 128), 640)
            c = cols[:, lanes]
            kc[core * 3 + i, rows, :] = (dot(thi[rows, :], c) + dot(tlo[rows, :], c)).astype(BF16)
            return 0

        lax.fori_loop(0, 2, block, 0)
        kc_copy(i).start()

    own_chunk.wait()
    pl.semaphore_wait(barrier, 14)

    for h in range(2):
        target = h * 4 + lax.rem(z_low, 2) * 2 + lax.div(z_low, 2)

        @pl.when(target != k)
        def _():
            remote(block_rows.at[pl.ds(h * 16, 16)], chunks.at[k], chunk_send.at[h], chunk_recv, (col, target)).start()

    for d in (2, -2):
        pl.semaphore_signal(hello, inc=1, device_id=at_z(d), device_id_type=MESH)
    for d in range(1, 8):
        remote(phase, angles.at[k], ang_send, ang_recv, at_k(d)).start()

    basis_copy.wait()
    lax.fori_loop(0, 10, make_rows, 0)
    own_phase.wait()
    pl.semaphore_wait(hello, 2)

    def send_own(hops):
        for d in hops:
            here, there = unit_to_z(0, d)
            remote(held.at[here], held.at[there], near_send, unit_recv.at[lax.div(there, 4)], at_z(d)).start()

    @pl.when(hub)
    def _():
        chunks[k] = block_rows[pl.ds(pl.multiple_of(half * 16, 16), 16), :]
        await_all(chunks.at[pl.ds(0, 7)], chunk_recv)
        both = jnp.concatenate([chunks[i] + chunks[i + 4] for i in range(4)], axis=1)
        apart = jnp.concatenate([chunks[i] - chunks[i + 4] for i in range(4)], axis=1)
        both = both - jnp.sum(both, axis=1, keepdims=True) * (2.0 / FRAMES)
        rest = jnp.zeros((16, FP - FREQS), F32)
        held[xx] = jnp.concatenate([both, rest, apart, rest], axis=1).astype(BF16)
        send_own(NEAR)

    def arrived(rel):
        here = rel * 4 + xx
        remote(held.at[here], held.at[here], near_send, unit_recv.at[rel], at_z(1)).wait_recv()

    def relay_copies(rel):
        copies = []
        for d in (-3, -2, -1) if rel == 1 else (4, 3, 2, 1):
            here, there = unit_to_z(rel, d)
            copies.append(remote(held.at[here], held.at[there], relay_send, unit_recv.at[lax.div(there, 4)], at_z(d)))
        return copies

    def x_copies(rel, hops=(2, 1, 3)):
        here = rel * 4 + xx
        return [remote(held.at[here], held.at[here], x_send, x_recv.at[rel // 2], at_x(d)) for d in hops]

    def relay(rel):
        for copy in relay_copies(rel):
            copy.start()

    def forward(rel):
        for copy in x_copies(rel):
            copy.start()

    @pl.when(hub)
    def _():
        forward(0)

    cols[pl.ds(FRAMES, TP - FRAMES), :] = jnp.zeros((TP - FRAMES, 768), BF16)
    series_copy.wait()
    norm_cols()

    turned = lax.rem(lax.div(behind + 1, 2), 2)

    def neighbour(rel):
        arrived(rel)
        relay(rel)
        forward(rel)

    transform_cols(0)

    @pl.when(jnp.logical_not(hub))
    def _():
        arrived(0)
        forward(0)

    @pl.when(hub & (turned == 0))
    def _():
        neighbour(1)
        neighbour(3)

    @pl.when(hub & (turned == 1))
    def _():
        neighbour(3)
        neighbour(1)

    transform_cols(1)

    @pl.when(jnp.logical_not(hub))
    def _():
        arrived(1)
        forward(1)

    transform_cols(2)

    @pl.when(jnp.logical_not(hub))
    def _():
        arrived(3)
        x_copies(3, (2,))[0].start()
        arrived(2)
        x_copies(2, (2,))[0].start()
        for rel in (3, 2):
            for copy in x_copies(rel, (1, 3)):
                copy.start()

    @pl.when(hub)
    def _():
        arrived(2)
        forward(2)

    await_all(angles.at[pl.ds(0, 7)], ang_recv)
    turn = jnp.concatenate([angles[i] for i in range(8)] + [jnp.zeros((SURR, FP - FREQS), jnp.int32)], axis=1)
    digits = jnp.concatenate([lax.div(turn, 32), lax.rem(turn, 32)], axis=0).astype(F32).astype(BF16)
    source = lax.broadcasted_iota(jnp.int32, (FP, FP), 0) + 1
    place = lax.broadcasted_iota(jnp.int32, (FP, FP), 1)
    freq = 2 * place + jnp.where(
        place < 256, 2, jnp.where(place < 512, -511, jnp.where(place <= LAST, -510, jnp.where(place < FREQS, -599, FRAMES)))
    )
    moved = dot(digits, jnp.where(source == freq, 1.0, 0.0).astype(BF16))
    angle = (moved[:SURR] * 32.0 + moved[SURR:]) * (2.0 * math.pi / FRAMES)
    lane = lax.broadcasted_iota(jnp.int32, (SURR, FP), 1)
    weight = jnp.where(lane < FREQS, jnp.where(lane == LAST, 0.5, 1.0), 0.0).astype(F32)
    cos_phase = jnp.cos(angle) * weight
    sin_phase = jnp.sin(angle) * weight
    lane1 = lax.broadcasted_iota(jnp.int32, (1, FP), 1)
    inner = ((lane1 < FREQS) & (lane1 != LAST)).astype(F32)
    even_lane = lax.rem(lax.broadcasted_iota(jnp.int32, (128, 256), 1), 128) <= LAST - 512
    lane128 = lax.broadcasted_iota(jnp.int32, (256, 128), 1)
    row16 = lax.rem(lax.broadcasted_iota(jnp.int32, (256, 128), 0), 16)

    def spectra(h):
        await_all(held.at[pl.ds(0, 6)], x_recv.at[h])
        rows = pl.ds(128 * h, 128)
        both = held[8 * h : 8 * h + 8, :, 0:FP].reshape(128, FP)
        apart = held[8 * h : 8 * h + 8, :, FP:TP].reshape(128, FP)

        def spectrum(x, start):
            table = pl.ds(start, 256)
            return dot_t(x, thi[table, 0:FP]) + dot_t(x, tlo[table, 0:FP])

        for start in (0, 768):
            spec[rows, start : start + 256] = spectrum(both, start)
            spec[rows, start + 256 : start + 512] = spectrum(apart, start + 256)
        spec[rows, 512:768] = jnp.where(even_lane, spectrum(both, 512), spectrum(apart, 512))

    def halves(rows):
        sc = spec[rows, 0:FP]
        ss = jnp.concatenate([spec[rows, 768:TP], spec[rows, FP:768]], axis=1)
        return sc, ss

    def power(h):
        sc, ss = halves(pl.ds(128 * h, 128))
        inside = jnp.sum((sc * sc + ss * ss) * inner, axis=1, keepdims=True)
        return inside, jnp.sum(jnp.where(lane1 == LAST, sc, 0.0), axis=1, keepdims=True)

    def rotate(h, s):
        sc, ss = halves(pl.ds(128 * h, 128))
        cp = cos_phase[s : s + 1, :]
        sp = sin_phase[s : s + 1, :]
        rows = pl.ds(s * 256 + 128 * h, 128)
        rot[rows, 0:FP] = (sc * cp + ss * sp).astype(BF16)
        turned_back = (ss * cp - sc * sp).astype(BF16)
        rot[rows, 768:TP] = turned_back[:, 0:512]
        rot[rows, FP:768] = turned_back[:, 512:FP]

    spectra(0)
    powers = [power(0)]
    for s in range(SURR):
        rotate(0, s)
    await_all(kc.at[pl.ds(0, 3)], kc_recv)
    spectra(1)
    powers.append(power(1))
    scales = []
    for s in range(SURR):
        energy = []
        for inside, last in powers:
            end = 2.0 * cos_phase[s : s + 1, LAST : LAST + 1] * last
            energy.append(inside * (2.0 / FRAMES) + end * end * (1.0 / FRAMES))
        scales.append(lax.rsqrt(jnp.concatenate(energy, axis=0) + EPS) * (math.sqrt(FRAMES) * 2.0 / FRAMES))
    placed = jnp.zeros((256, 128), F32)
    for s in range(SURR):
        rotate(1, s)
        rows = pl.ds(s * 256, 256)
        for j in range(6):
            score = jnp.abs(dot(rot[rows, :], kc[j]))
            score = jnp.maximum(score[:, :128], score[:, 128:])
            tops = score if j == 0 else jnp.maximum(tops, score)
        placed = jnp.where(lane128 == row16 + 16 * s, jnp.max(tops, axis=1, keepdims=True) * scales[s], placed)
    found = jnp.max(placed.reshape(16, 16, 128), axis=1)
    own_top[...] = jnp.max(found, axis=0, keepdims=True)
    for n, (dx, dk) in enumerate(PLANE):
        remote(own_top, top1.at[n], t1_send, t1_recv, at_xk(dx, dk)).start()
    for n in range(16):
        row = (n % 4) * 4 + lax.rem(behind + n // 4, 4)
        mine[pl.ds(row, 1), :] = found[n : n + 1, :]
    await_all(top1, t1_recv)
    wide_top[...] = jnp.maximum(own_top[...], jnp.max(top1[...], axis=0))
    for n, d in enumerate(RING):
        remote(wide_top, top2.at[n], t2_send, t2_recv, at_z(d)).start()
    for d in range(1, 8):
        remote(mine, parts.at[k], part_send, part_recv, at_k(d)).start()
    parts[k] = mine[...]
    await_all(parts.at[pl.ds(0, 7)], part_recv)
    lane16 = lax.broadcasted_iota(jnp.int32, (16, 128), 1)
    for s in range(SURR):
        full = jnp.zeros((16, 128), F32)
        for kk in range(8):
            place = (kk % 2 * 2 + kk % 4 // 2) * 32 + (kk // 4) * 16
            moved = pltpu.roll(parts[kk], (place - 16 * s) % 128, 1)
            full = jnp.where((lane16 >= place) & (lane16 < place + 16), moved, full)
        out_tile[pl.ds(s * 16, 16), :] = full
    await_all(top2, t2_recv)
    every = jnp.maximum(wide_top[...], jnp.max(top2[...], axis=0))
    row_lane = lax.broadcasted_iota(jnp.int32, (1, 128), 1)
    result = jnp.zeros((1, 128), F32)
    for s in range(SURR):
        inside = (row_lane >= 16 * s) & (row_lane < 16 * s + 16)
        result = jnp.where(row_lane == s, jnp.max(jnp.where(inside, every, 0.0), axis=1, keepdims=True), result)
    out_peak[...] = result

    for h in range(2):
        target = h * 4 + lax.rem(z_low, 2) * 2 + lax.div(z_low, 2)

        @pl.when(target != k)
        def _():
            remote(block_rows.at[pl.ds(h * 16, 16)], chunks.at[k], chunk_send.at[h], chunk_recv, (col, target)).wait_send()

    @pl.when(hub)
    def _():
        await_sent(held.at[pl.ds(0, 8)], near_send)
        await_sent(held.at[pl.ds(0, 7)], relay_send)

    await_sent(angles.at[pl.ds(0, 7)], ang_send)
    await_sent(held.at[pl.ds(0, 12)], x_send)
    await_sent(kc.at[pl.ds(0, 3)], kc_send)
    await_sent(parts.at[pl.ds(0, 7)], part_send)
    await_sent(top1, t1_send)
    await_sent(top2, t2_send)


def body(series, slab_series, phase_index, basis):
    dma = pltpu.SemaphoreType.DMA
    vmem = pl.BlockSpec(memory_space=pltpu.VMEM)
    hbm = pl.BlockSpec(memory_space=pl.ANY)
    tile, peak = pl.pallas_call(
        kernel,
        out_shape=(pltpu.VMEM((64, 128), F32), pltpu.VMEM((1, 128), F32)),
        in_specs=[hbm, hbm, hbm, hbm],
        out_specs=(vmem, vmem),
        scratch_shapes=[
            pltpu.VMEM((TP, 768), BF16),
            pltpu.VMEM((4, FP, 128), F32),
            pltpu.VMEM((TP, TP), BF16),
            pltpu.VMEM((TP, TP), BF16),
            pltpu.VMEM((6, TP, 256), BF16),
            pltpu.VMEM((16, 16, TP), BF16),
            pltpu.VMEM((32, 150), F32),
            pltpu.VMEM((8, 16, 150), F32),
            pltpu.VMEM((8, SURR, 75), jnp.int32),
            pltpu.VMEM((256, TP), F32),
            pltpu.VMEM((1024, TP), BF16),
            pltpu.VMEM((16, 128), F32),
            pltpu.VMEM((8, 16, 128), F32),
            pltpu.VMEM((1, 128), F32),
            pltpu.VMEM((31, 1, 128), F32),
            pltpu.VMEM((1, 128), F32),
            pltpu.VMEM((15, 1, 128), F32),
            dma((2,)), dma, dma, dma((2,)), dma, dma, dma, dma, dma, dma, dma((2,)), dma((4,)),
            dma, dma, dma, dma, dma, dma, dma, dma, pltpu.SemaphoreType.REGULAR,
        ],
        compiler_params=pltpu.CompilerParams(
            collective_id=0, has_side_effects=True, vmem_limit_bytes=56 * 1024 * 1024
        ),
        name="surrogate_peaks",
    )(series, slab_series.T, phase_index, basis)
    return tile.reshape(SURR, 2048)[:, :, None], peak[0, :SURR]


def solution(mesh):
    basis = basis_tables()

    def run(series, slab_series, phase_index):
        placed = (P(None, "col"), P("tm", "col"), P(None, "tm"), P())
        step = jax.shard_map(
            body, mesh=mesh, in_specs=placed, out_specs=(P(None, None, "col"), P()), check_vma=False
        )
        return step(series, slab_series, phase_index, jnp.asarray(basis))

    return run
```

```python
import functools
import math

import jax
import jax.numpy as jnp
import numpy as np
from jax import lax
from jax.experimental import pallas as pl
from jax.experimental.pallas import tpu as pltpu
from jax.sharding import PartitionSpec as P

FRAMES = 1200
FREQS = 600
FP = 640
TP = 1280
SURR = 4
COLS = 1536
EPS = 1e-6
F32 = jnp.float32
BF16 = jnp.bfloat16
MESH = pl.DeviceIdType.MESH
NEAR = (4, -4, 3, -3, 2, -2, 1, -1)
RING = (8, 7, -7, 6, -6, 5, -5, 4, -4, 3, -3, 2, -2, 1, -1)
PLANE = tuple((dx, dk) for dx in (2, 1, 3, 0) for dk in (4, 5, 3, 2, 6, 7, 1, 0) if (dx, dk) != (0, 0))


ORDER = np.concatenate([np.arange(2, 514, 2), np.arange(1, 513, 2), np.arange(514, 601, 2), np.arange(513, 600, 2)])
LAST = 555


def basis_tables():
    freq = np.concatenate([ORDER, np.ones(FP - FREQS, ORDER.dtype)])[:, None]
    lane = np.arange(128)[None, :]
    fine = 2.0 * np.pi * ((freq * lane) % FRAMES) / FRAMES
    step = np.broadcast_to(2.0 * np.pi * ((freq * 128) % FRAMES) / FRAMES, fine.shape)
    return np.stack([np.cos(fine), np.sin(fine), np.cos(step), np.sin(step)]).astype(np.float32)


def dot(a, b):
    return lax.dot_general(a, b, (((1,), (0,)), ((), ())), preferred_element_type=F32)


def dot_t(a, b):
    return lax.dot_general(a, b, (((1,), (1,)), ((), ())), preferred_element_type=F32)


def kernel(
    series, slab, phase, basis, out_tile, out_peak,
    cols, bas, thi, tlo, kc, held, block_rows, chunks, angles, spec, rot, mine, parts, own_top, top1, wide_top, top2,
    own_sem, col_sem, bas_sem, chunk_send, chunk_recv, ang_send, ang_recv, near_send, relay_send, x_send, x_recv, unit_recv,
    kc_send, kc_recv, part_send, part_recv, t1_send, t1_recv, t2_send, t2_recv, hello,
):
    col = lax.axis_index("col")
    k = lax.axis_index("tm")
    xx = lax.div(col, 16)
    z = lax.rem(col, 16)
    residue = lax.rem(k, 2) * 2 + lax.div(lax.rem(k, 4), 2)
    half = lax.div(k, 4)
    core = lax.rem(k, 2)
    z_low = lax.rem(z, 4)
    hub = z_low == residue

    def at_z(d):
        return (xx * 16 + lax.rem(z + d + 16, 16), k)

    def at_x(d):
        return (lax.rem(xx + d, 4) * 16 + z, k)

    def at_xk(dx, dk):
        return (lax.rem(xx + dx, 4) * 16 + z, lax.rem(k + dk, 8))

    def at_k(d):
        return (col, lax.rem(k + d, 8))

    def remote(src, dst, send, recv, dev):
        return pltpu.make_async_remote_copy(
            src_ref=src, dst_ref=dst, send_sem=send, recv_sem=recv, device_id=dev, device_id_type=MESH
        )

    def await_sent(ref, sem):
        remote(ref, ref, sem, sem, at_k(1)).wait_send()

    def await_all(ref, sem):
        remote(ref, ref, sem, sem, at_k(1)).wait_recv()

    def behind_of(d):
        return lax.div(lax.rem(z + d - residue + 32, 16), 4)

    behind = behind_of(0)

    def unit_to_z(rel, d):
        here = rel * 4 + xx
        there = lax.rem(behind + rel - behind_of(d) + 8, 4) * 4 + xx
        return here, there

    series_copy = pltpu.make_async_copy(
        series.at[:, pl.ds(pl.multiple_of(core * 768, 256), 768)], cols.at[pl.ds(0, FRAMES)], col_sem
    )
    basis_copy = pltpu.make_async_copy(basis, bas, bas_sem)
    own_phase = pltpu.make_async_copy(phase, angles.at[k], own_sem.at[0])
    own_chunk = pltpu.make_async_copy(slab, block_rows, own_sem.at[1])

    barrier = pltpu.get_barrier_semaphore()
    peers = [at_k(d) for d in range(1, 8)] + [at_x(d) for d in range(1, 4)] + [at_z(d) for d in (2, -2, 1, -1)]
    for dev in peers:
        pl.semaphore_signal(barrier, inc=1, device_id=dev, device_id_type=MESH)

    own_phase.start()
    own_chunk.start()
    basis_copy.start()
    series_copy.start()

    def make_rows(i, _):
        at = pl.multiple_of(i * 64, 64)
        sin_at = pl.multiple_of(FP + lax.rem(i + 2, 10) * 64, 64)
        c = bas[0, pl.ds(at, 64), :]
        s = bas[1, pl.ds(at, 64), :]
        sc = bas[2, pl.ds(at, 64), :]
        ss = bas[3, pl.ds(at, 64), :]
        for a in range(10):
            lanes = pl.ds(a * 128, 128)
            for rows, val in ((pl.ds(at, 64), c), (pl.ds(sin_at, 64), s)):
                hi = val.astype(BF16)
                thi[rows, lanes] = hi
                tlo[rows, lanes] = (val - hi.astype(F32)).astype(BF16)
            c, s = c * sc - s * ss, s * sc + c * ss
        return 0

    def norm_cols():
        def total(i, acc):
            x = cols[pl.ds(pl.multiple_of(i * 80, 16), 80), :].astype(F32)
            return acc + jnp.sum(x.reshape(10, 8, 768), axis=0)

        mean = jnp.sum(lax.fori_loop(0, 15, total, jnp.zeros((8, 768), F32)), axis=0, keepdims=True) * (1.0 / FRAMES)

        def squares(i, acc):
            x = cols[pl.ds(pl.multiple_of(i * 80, 16), 80), :].astype(F32) - mean
            return acc + jnp.sum((x * x).reshape(10, 8, 768), axis=0)

        scale = lax.rsqrt(jnp.sum(lax.fori_loop(0, 15, squares, jnp.zeros((8, 768), F32)), axis=0, keepdims=True) + EPS)

        def write(i, _):
            rows = pl.ds(pl.multiple_of(i * 80, 16), 80)
            cols[rows, :] = ((cols[rows, :].astype(F32) - mean) * scale).astype(BF16)
            return 0

        lax.fori_loop(0, 15, write, 0)

    def kc_copy(i):
        block = kc.at[core * 3 + i]
        return remote(block, block, kc_send, kc_recv, (col, k + 1 - 2 * core))

    def transform_cols(i):
        lanes = pl.ds(i * 256, 256)

        def block(b, _):
            rows = pl.ds(pl.multiple_of(b * 640, 128), 640)
            c = cols[:, lanes]
            kc[core * 3 + i, rows, :] = (dot(thi[rows, :], c) + dot(tlo[rows, :], c)).astype(BF16)
            return 0

        lax.fori_loop(0, 2, block, 0)
        kc_copy(i).start()

    own_chunk.wait()
    pl.semaphore_wait(barrier, 14)

    for h in range(2):
        target = h * 4 + lax.rem(z_low, 2) * 2 + lax.div(z_low, 2)

        @pl.when(target != k)
        def _():
            remote(block_rows.at[pl.ds(h * 16, 16)], chunks.at[k], chunk_send.at[h], chunk_recv, (col, target)).start()

    for d in (2, -2):
        pl.semaphore_signal(hello, inc=1, device_id=at_z(d), device_id_type=MESH)
    for d in range(1, 8):
        remote(phase, angles.at[k], ang_send, ang_recv, at_k(d)).start()

    basis_copy.wait()
    lax.fori_loop(0, 10, make_rows, 0)
    own_phase.wait()
    pl.semaphore_wait(hello, 2)

    def send_own(hops):
        for d in hops:
            here, there = unit_to_z(0, d)
            remote(held.at[here], held.at[there], near_send, unit_recv.at[lax.div(there, 4)], at_z(d)).start()

    @pl.when(hub)
    def _():
        chunks[k] = block_rows[pl.ds(pl.multiple_of(half * 16, 16), 16), :]
        await_all(chunks.at[pl.ds(0, 7)], chunk_recv)
        both = jnp.concatenate([chunks[i] + chunks[i + 4] for i in range(4)], axis=1)
        apart = jnp.concatenate([chunks[i] - chunks[i + 4] for i in range(4)], axis=1)
        both = both - jnp.sum(both, axis=1, keepdims=True) * (2.0 / FRAMES)
        rest = jnp.zeros((16, FP - FREQS), F32)
        held[xx] = jnp.concatenate([both, rest, apart, rest], axis=1).astype(BF16)
        send_own(NEAR)

    def arrived(rel):
        here = rel * 4 + xx
        remote(held.at[here], held.at[here], near_send, unit_recv.at[rel], at_z(1)).wait_recv()

    def relay_copies(rel):
        copies = []
        for d in (-3, -2, -1) if rel == 1 else (4, 3, 2, 1):
            here, there = unit_to_z(rel, d)
            copies.append(remote(held.at[here], held.at[there], relay_send, unit_recv.at[lax.div(there, 4)], at_z(d)))
        return copies

    def x_copies(rel, hops=(2, 1, 3)):
        here = rel * 4 + xx
        return [remote(held.at[here], held.at[here], x_send, x_recv.at[rel // 2], at_x(d)) for d in hops]

    def relay(rel):
        for copy in relay_copies(rel):
            copy.start()

    def forward(rel):
        for copy in x_copies(rel):
            copy.start()

    @pl.when(hub)
    def _():
        forward(0)

    cols[pl.ds(FRAMES, TP - FRAMES), :] = jnp.zeros((TP - FRAMES, 768), BF16)
    series_copy.wait()
    norm_cols()

    turned = lax.rem(lax.div(behind + 1, 2), 2)

    def neighbour(rel):
        arrived(rel)
        relay(rel)
        forward(rel)

    transform_cols(0)

    @pl.when(jnp.logical_not(hub))
    def _():
        arrived(0)
        forward(0)

    @pl.when(hub & (turned == 0))
    def _():
        neighbour(1)
        neighbour(3)

    @pl.when(hub & (turned == 1))
    def _():
        neighbour(3)
        neighbour(1)

    transform_cols(1)

    @pl.when(jnp.logical_not(hub))
    def _():
        arrived(1)
        forward(1)

    transform_cols(2)

    @pl.when(jnp.logical_not(hub))
    def _():
        arrived(3)
        x_copies(3, (2,))[0].start()
        arrived(2)
        x_copies(2, (2,))[0].start()
        for rel in (3, 2):
            for copy in x_copies(rel, (1, 3)):
                copy.start()

    @pl.when(hub)
    def _():
        arrived(2)
        forward(2)

    await_all(angles.at[pl.ds(0, 7)], ang_recv)
    turn = jnp.concatenate([angles[i] for i in range(8)] + [jnp.zeros((SURR, FP - FREQS), jnp.int32)], axis=1)
    digits = jnp.concatenate([lax.div(turn, 32), lax.rem(turn, 32)], axis=0).astype(F32).astype(BF16)
    source = lax.broadcasted_iota(jnp.int32, (FP, FP), 0) + 1
    place = lax.broadcasted_iota(jnp.int32, (FP, FP), 1)
    freq = 2 * place + jnp.where(
        place < 256, 2, jnp.where(place < 512, -511, jnp.where(place <= LAST, -510, jnp.where(place < FREQS, -599, FRAMES)))
    )
    moved = dot(digits, jnp.where(source == freq, 1.0, 0.0).astype(BF16))
    angle = (moved[:SURR] * 32.0 + moved[SURR:]) * (2.0 * math.pi / FRAMES)
    lane = lax.broadcasted_iota(jnp.int32, (SURR, FP), 1)
    weight = jnp.where(lane < FREQS, jnp.where(lane == LAST, 0.5, 1.0), 0.0).astype(F32)
    cos_phase = jnp.cos(angle) * weight
    sin_phase = jnp.sin(angle) * weight
    lane1 = lax.broadcasted_iota(jnp.int32, (1, FP), 1)
    inner = ((lane1 < FREQS) & (lane1 != LAST)).astype(F32)
    even_lane = lax.rem(lax.broadcasted_iota(jnp.int32, (128, 256), 1), 128) <= LAST - 512
    lane128 = lax.broadcasted_iota(jnp.int32, (256, 128), 1)
    row16 = lax.rem(lax.broadcasted_iota(jnp.int32, (256, 128), 0), 16)

    def spectra(h):
        await_all(held.at[pl.ds(0, 6)], x_recv.at[h])
        rows = pl.ds(128 * h, 128)
        both = held[8 * h : 8 * h + 8, :, 0:FP].reshape(128, FP)
        apart = held[8 * h : 8 * h + 8, :, FP:TP].reshape(128, FP)

        def spectrum(x, start):
            table = pl.ds(start, 256)
            return dot_t(x, thi[table, 0:FP]) + dot_t(x, tlo[table, 0:FP])

        for start in (0, 768):
            spec[rows, start : start + 256] = spectrum(both, start)
            spec[rows, start + 256 : start + 512] = spectrum(apart, start + 256)
        spec[rows, 512:768] = jnp.where(even_lane, spectrum(both, 512), spectrum(apart, 512))

    def halves(rows):
        sc = spec[rows, 0:FP]
        ss = jnp.concatenate([spec[rows, 768:TP], spec[rows, FP:768]], axis=1)
        return sc, ss

    def power(h):
        sc, ss = halves(pl.ds(128 * h, 128))
        inside = jnp.sum((sc * sc + ss * ss) * inner, axis=1, keepdims=True)
        return inside, jnp.sum(jnp.where(lane1 == LAST, sc, 0.0), axis=1, keepdims=True)

    def rotate(h, s):
        sc, ss = halves(pl.ds(128 * h, 128))
        cp = cos_phase[s : s + 1, :]
        sp = sin_phase[s : s + 1, :]
        rows = pl.ds(s * 256 + 128 * h, 128)
        rot[rows, 0:FP] = (sc * cp + ss * sp).astype(BF16)
        turned_back = (ss * cp - sc * sp).astype(BF16)
        rot[rows, 768:TP] = turned_back[:, 0:512]
        rot[rows, FP:768] = turned_back[:, 512:FP]

    spectra(0)
    powers = [power(0)]
    for s in range(SURR):
        rotate(0, s)
    await_all(kc.at[pl.ds(0, 3)], kc_recv)
    spectra(1)
    powers.append(power(1))
    scales = []
    for s in range(SURR):
        energy = []
        for inside, last in powers:
            end = 2.0 * cos_phase[s : s + 1, LAST : LAST + 1] * last
            energy.append(inside * (2.0 / FRAMES) + end * end * (1.0 / FRAMES))
        scales.append(lax.rsqrt(jnp.concatenate(energy, axis=0) + EPS) * (math.sqrt(FRAMES) * 2.0 / FRAMES))
    placed = jnp.zeros((256, 128), F32)
    for pair in range(2):
        for s in (2 * pair, 2 * pair + 1):
            rotate(1, s)
        rows = pl.ds(pair * 512, 512)
        for j in range(6):
            score = jnp.abs(dot(rot[rows, :], kc[j]))
            score = jnp.maximum(score[:, :128], score[:, 128:])
            tops = score if j == 0 else jnp.maximum(tops, score)
        for s in (2 * pair, 2 * pair + 1):
            own = tops[256 * (s % 2) : 256 * (s % 2) + 256]
            placed = jnp.where(lane128 == row16 + 16 * s, jnp.max(own, axis=1, keepdims=True) * scales[s], placed)
    found = jnp.max(placed.reshape(16, 16, 128), axis=1)
    for n in range(16):
        row = (n % 4) * 4 + lax.rem(behind + n // 4, 4)
        mine[pl.ds(row, 1), :] = found[n : n + 1, :]

    own_top[...] = jnp.max(mine[...], axis=0, keepdims=True)
    for n, (dx, dk) in enumerate(PLANE):
        remote(own_top, top1.at[n], t1_send, t1_recv, at_xk(dx, dk)).start()
    for d in range(1, 8):
        remote(mine, parts.at[k], part_send, part_recv, at_k(d)).start()
    parts[k] = mine[...]
    await_all(top1, t1_recv)
    wide_top[...] = jnp.maximum(own_top[...], jnp.max(top1[...], axis=0))
    for n, d in enumerate(RING):
        remote(wide_top, top2.at[n], t2_send, t2_recv, at_z(d)).start()
    await_all(parts.at[pl.ds(0, 7)], part_recv)
    lane16 = lax.broadcasted_iota(jnp.int32, (16, 128), 1)
    for s in range(SURR):
        full = jnp.zeros((16, 128), F32)
        for kk in range(8):
            place = (kk % 2 * 2 + kk % 4 // 2) * 32 + (kk // 4) * 16
            moved = pltpu.roll(parts[kk], (place - 16 * s) % 128, 1)
            full = jnp.where((lane16 >= place) & (lane16 < place + 16), moved, full)
        out_tile[pl.ds(s * 16, 16), :] = full
    await_all(top2, t2_recv)
    every = jnp.maximum(wide_top[...], jnp.max(top2[...], axis=0))
    row_lane = lax.broadcasted_iota(jnp.int32, (1, 128), 1)
    result = jnp.zeros((1, 128), F32)
    for s in range(SURR):
        inside = (row_lane >= 16 * s) & (row_lane < 16 * s + 16)
        result = jnp.where(row_lane == s, jnp.max(jnp.where(inside, every, 0.0), axis=1, keepdims=True), result)
    out_peak[...] = result

    for h in range(2):
        target = h * 4 + lax.rem(z_low, 2) * 2 + lax.div(z_low, 2)

        @pl.when(target != k)
        def _():
            remote(block_rows.at[pl.ds(h * 16, 16)], chunks.at[k], chunk_send.at[h], chunk_recv, (col, target)).wait_send()

    @pl.when(hub)
    def _():
        await_sent(held.at[pl.ds(0, 8)], near_send)
        await_sent(held.at[pl.ds(0, 7)], relay_send)

    await_sent(angles.at[pl.ds(0, 7)], ang_send)
    await_sent(held.at[pl.ds(0, 12)], x_send)
    await_sent(kc.at[pl.ds(0, 3)], kc_send)
    await_sent(parts.at[pl.ds(0, 7)], part_send)
    await_sent(top1, t1_send)
    await_sent(top2, t2_send)


def body(series, slab_series, phase_index, basis):
    dma = pltpu.SemaphoreType.DMA
    vmem = pl.BlockSpec(memory_space=pltpu.VMEM)
    hbm = pl.BlockSpec(memory_space=pl.ANY)
    tile, peak = pl.pallas_call(
        kernel,
        out_shape=(pltpu.VMEM((64, 128), F32), pltpu.VMEM((1, 128), F32)),
        in_specs=[hbm, hbm, hbm, hbm],
        out_specs=(vmem, vmem),
        scratch_shapes=[
            pltpu.VMEM((TP, 768), BF16),
            pltpu.VMEM((4, FP, 128), F32),
            pltpu.VMEM((TP, TP), BF16),
            pltpu.VMEM((TP, TP), BF16),
            pltpu.VMEM((6, TP, 256), BF16),
            pltpu.VMEM((16, 16, TP), BF16),
            pltpu.VMEM((32, 150), F32),
            pltpu.VMEM((8, 16, 150), F32),
            pltpu.VMEM((8, SURR, 75), jnp.int32),
            pltpu.VMEM((256, TP), F32),
            pltpu.VMEM((1024, TP), BF16),
            pltpu.VMEM((16, 128), F32),
            pltpu.VMEM((8, 16, 128), F32),
            pltpu.VMEM((1, 128), F32),
            pltpu.VMEM((31, 1, 128), F32),
            pltpu.VMEM((1, 128), F32),
            pltpu.VMEM((15, 1, 128), F32),
            dma((2,)), dma, dma, dma((2,)), dma, dma, dma, dma, dma, dma, dma((2,)), dma((4,)),
            dma, dma, dma, dma, dma, dma, dma, dma, pltpu.SemaphoreType.REGULAR,
        ],
        compiler_params=pltpu.CompilerParams(
            collective_id=0, has_side_effects=True, vmem_limit_bytes=56 * 1024 * 1024
        ),
        name="surrogate_peaks",
    )(series, slab_series.T, phase_index, basis)
    return tile.reshape(SURR, 2048)[:, :, None], peak[0, :SURR]


def solution(mesh):
    basis = basis_tables()

    def run(series, slab_series, phase_index):
        placed = (P(None, "col"), P("tm", "col"), P(None, "tm"), P())
        step = jax.shard_map(
            body, mesh=mesh, in_specs=placed, out_specs=(P(None, None, "col"), P()), check_vma=False
        )
        return step(series, slab_series, phase_index, jnp.asarray(basis))

    return run
```
